32 devices in a mesh: chan: 8 (over z, x), tm: 4 (over y, core).
Axes of the slice: x: 2, y: 2, z: 4, core: 2. Of those that a mesh axis runs over, the one named last changes fastest.
Arguments:
- records: bfloat16 [1280, 16, 7680], P('chan', 'tm'), may hold values from -6 to 6
- valid_mask: int32 [8, 16], P('chan', 'tm'), may hold values 0 or 1
- band_limits: int32 [8, 2], P('chan'), may hold values from 0 to 321, as said below
Outputs:
- correlations: float32 [1280, 32, 128], P('chan', 'tm')
The draws below stay inside these ranges and needn't reach their ends.
Inputs may be any that keep to these rules, and one draw needn't show every extreme that they name: band_limits[b, 0] <= 289 and 1 <= band_limits[b, 1] - band_limits[b, 0] <= 32.
All inputs are finite; a program needn't handle non-finite values. No bound on the sum of `valid_mask` on one device may be relied on, other than what follows from the above.
Results may differ from the reference program's by a relative error of at most 0.013.
Values may be sent and summed in bfloat16 or wider, within the bound.
No kernel may reach another device: no remote copies, remote signals or barrier semaphores. Data moves between devices by JAX's collectives and lax.ppermute only.
A program may use at most 256 MiB of HBM per device.

```python
import math
import jax
import jax.numpy as jnp
from jax import lax

SAMPLES = 7680
BINS = 512
LAGS = 128
PAIRS = 32
REACH = 2
CH_DEV = 160
SEG_DEV = 4
BLOCKS = 8
CHANNELS = 1280
SEGMENTS = 16


def draw_band_limits(key, part):
    keys = jax.random.split(key, 4)
    highest_low = REACH * CH_DEV + 1 - PAIRS
    lowest = jax.random.randint(keys[0], (BLOCKS,), 0, highest_low + 1)
    spread = jax.random.randint(keys[1], (BLOCKS,), 1, PAIRS + 1)
    far_block = jax.random.randint(keys[2], (), 0, BLOCKS)
    near_block = (far_block + 1 + jax.random.randint(keys[3], (), 0, BLOCKS - 1)) % BLOCKS
    position = jnp.arange(BLOCKS)
    lowest = jnp.where(position == far_block, highest_low, jnp.where(position == near_block, 0, lowest))
    spread = jnp.where(position == far_block, PAIRS, spread)
    return jnp.stack([lowest, lowest + spread], axis=1).astype(jnp.int32)


def plant(values, own_key, low, top_value):
    dims = values.shape
    spot = [jax.random.randint(jax.random.fold_in(own_key, axis), (), 0, dims[axis]) for axis in range(len(dims))]
    values = values.at[tuple(spot)].set(low)
    longest = dims.index(max(dims))
    spot[longest] = (spot[longest] + 1) % dims[longest]
    return values.at[tuple(spot)].set(top_value)


def level_of(own_key, extent, cuts, least, top_value):
    level, own = 1.0, jax.random.fold_in(own_key, 6)
    for axis_at, parts in cuts:
        steps = jnp.exp(jax.random.uniform(jax.random.fold_in(own, axis_at), (parts,), jnp.float32, least / len(cuts), top_value / len(cuts)))
        level = level * jnp.repeat(steps, extent[axis_at] // parts).reshape([-1 if axis == axis_at else 1 for axis in range(len(extent))])
    return level


def bell_draw(rng, extent, scale, reach, pieces=(), kind=jnp.bfloat16):
    gain = level_of(rng, extent, pieces, -0.22, 0.18) if pieces else 1.0
    drawn = jax.random.normal(rng, extent, jnp.float32) * scale * gain
    return jnp.minimum(jnp.maximum(drawn, -reach), reach).astype(kind)


def setup_inputs(seed: int = 0) -> dict:
    key_of = jax.random.split(jax.random.key(seed), 4)
    return {
        "records": bell_draw(key_of[0], (CHANNELS, SEGMENTS, SAMPLES), 1.0, 6.0, ((0, 8), (1, 4))),
        "valid_mask": plant((jax.random.randint(key_of[1], (BLOCKS, SEGMENTS), 0, 2) < 1).astype(jnp.int32), jax.random.fold_in(key_of[1], 1), 0, 1),
        "band_limits": draw_band_limits(jax.random.fold_in(key_of[3], 71), 0),
    }


def dft_table_of(samples, bins):
    times = jnp.arange(samples, dtype=jnp.int32)[:, None]
    freqs = 32 + jnp.arange(bins, dtype=jnp.int32)[None, :]
    phase = (times * freqs % samples).astype(jnp.float32) * (2.0 * math.pi / samples)
    return jnp.concatenate([jnp.cos(phase), -jnp.sin(phase)], axis=1).astype(jnp.bfloat16)

def lag_table_of(samples, bins, lags):
    freqs = 32 + jnp.arange(bins, dtype=jnp.int32)[:, None]
    shifts = (jnp.arange(lags, dtype=jnp.int32) - lags // 2 + samples) % samples
    phase = (freqs * shifts[None, :] % samples).astype(jnp.float32) * (2.0 * math.pi / samples)
    factor = 1.0 / math.sqrt(bins)
    return (jnp.concatenate([jnp.cos(phase), -jnp.sin(phase)], axis=0) * factor).astype(jnp.bfloat16)

def whiten(spectra, bins):
    real_part = spectra[:, :bins]
    imag_part = spectra[:, bins:]
    power_sum = real_part * real_part + imag_part * imag_part
    water_level = lax.optimization_barrier(jnp.mean(power_sum, axis=1, keepdims=True))
    inverse_amp = 1.0 / jnp.sqrt(power_sum + 0.1 * water_level + 1e-06)
    return jnp.concatenate([real_part * inverse_amp, imag_part * inverse_amp], axis=1).astype(jnp.bfloat16)

def cross_stack(extended, ext_weight, lowest, first_pair, pair_total, group_size, lag_table, block_size):
    seg_total = extended.shape[1]
    bins = extended.shape[2] // 2
    own_panel = extended[:block_size]
    own_weight = ext_weight[:block_size].astype(jnp.float32)

    def one_block(block_index):
        offsets = lowest + first_pair + block_index * 4 + jnp.arange(4, dtype=jnp.int32)
        partner = jax.vmap(lambda offset: lax.dynamic_slice_in_dim(extended, offset, block_size, 0))(offsets)
        partner_weight = jax.vmap(lambda offset: lax.dynamic_slice_in_dim(ext_weight, offset, block_size, 0))(offsets)
        mine = own_panel.astype(jnp.float32)[None]
        theirs = partner.astype(jnp.float32)
        weight = own_weight[None] * partner_weight.astype(jnp.float32)
        real_mix = (mine[..., :bins] * theirs[..., :bins] + mine[..., bins:] * theirs[..., bins:]) * weight[..., None]
        imag_mix = (mine[..., bins:] * theirs[..., :bins] - mine[..., :bins] * theirs[..., bins:]) * weight[..., None]
        cross_sum = jnp.concatenate([real_mix, imag_mix], axis=-1)
        cross_sum = cross_sum.reshape(4, block_size, seg_total // group_size, group_size, 2 * bins).sum(axis=3)
        cross_sum = cross_sum.astype(jnp.bfloat16)
        correlation = jnp.einsum('qcgf,fl->qcl', cross_sum.astype(jnp.float32), lag_table.astype(jnp.float32))
        pair_count = lax.optimization_barrier(jnp.sum(weight, axis=-1))
        return (correlation, pair_count)
    correlation, pair_count = lax.map(one_block, jnp.arange(pair_total // 4, dtype=jnp.int32))
    lags = correlation.shape[-1]
    correlation = jnp.transpose(correlation, (2, 0, 1, 3)).reshape(block_size, pair_total, lags)
    pair_count = jnp.transpose(pair_count, (2, 0, 1)).reshape(block_size, pair_total)
    return (correlation, pair_count)

def reference(records, valid_mask, band_limits):
    dft_table = dft_table_of(SAMPLES, BINS)
    lag_table = lag_table_of(SAMPLES, BINS, LAGS)

    def spectra_of(block_records):
        spectra = jnp.dot(block_records.reshape(CH_DEV * SEGMENTS, SAMPLES), dft_table, preferred_element_type=jnp.float32)
        return whiten(spectra, BINS).reshape(CH_DEV, SEGMENTS, 2 * BINS)
    white = lax.map(spectra_of, records.reshape(BLOCKS, CH_DEV, SEGMENTS, SAMPLES))
    padded = jnp.concatenate([white, jnp.zeros((REACH, CH_DEV, SEGMENTS, 2 * BINS), jnp.bfloat16)], axis=0)
    marks = jnp.concatenate([valid_mask, jnp.zeros((REACH, SEGMENTS), jnp.int32)], axis=0).astype(jnp.float32)

    def per_block(block):
        extended = lax.dynamic_slice_in_dim(padded, block, REACH + 1, 0).reshape((REACH + 1) * CH_DEV, SEGMENTS, 2 * BINS)
        ext_weight = jnp.repeat(lax.dynamic_slice_in_dim(marks, block, REACH + 1, 0), CH_DEV, axis=0)
        lowest = band_limits[block, 0]
        highest = band_limits[block, 1]
        summed, pair_count = cross_stack(extended, ext_weight, lowest, 0, PAIRS, SEG_DEV, lag_table, CH_DEV)
        inside = lowest + jnp.arange(PAIRS, dtype=jnp.int32) < highest
        result = summed / jnp.maximum(pair_count, 1.0)[..., None]
        return jnp.where(inside[None, :, None], result, jnp.zeros_like(result))
    output = lax.map(per_block, jnp.arange(BLOCKS, dtype=jnp.int32))
    return output.reshape(CHANNELS, PAIRS, LAGS)
```

```python
import functools
import math

import jax
import jax.numpy as jnp
import numpy as np
from jax import lax
from jax.experimental import pallas as pl
from jax.experimental.pallas import tpu as pltpu
from jax.sharding import PartitionSpec as P

BINS = 512
LAGS = 128
PAIRS = 32
REACH = 2
STEPS = 5


def bin_order(bins):
    return np.concatenate([np.arange(0, bins, 2), np.arange(1, bins, 2)])


def dft_table_of(samples, bins):
    times = np.arange(samples // 2, dtype=np.int64)[:, None]
    freqs = 32 + bin_order(bins)[None, :]
    phase = (times * freqs % samples) * (2.0 * math.pi / samples)
    half = bins // 2
    real, imag = np.cos(phase), -np.sin(phase)
    parts = [real[:, :half], imag[:, :half], real[:, half:], imag[:, half:]]
    return np.concatenate(parts, axis=1).astype(jnp.bfloat16)


def lag_table_of(samples, bins, lags):
    freqs = 32 + bin_order(bins)[:, None]
    shifts = (np.arange(lags) - lags // 2 + samples) % samples
    phase = (freqs * shifts[None, :] % samples) * (2.0 * math.pi / samples)
    factor = 1.0 / math.sqrt(bins)
    return (np.concatenate([np.cos(phase), -np.sin(phase)], axis=0) * factor).astype(jnp.bfloat16)


def spectra_kernel(valid_ref, first_ref, second_ref, table_ref, white_ref, acc):
    step = pl.program_id(0)
    channels, segs, width = first_ref.shape
    lane_tiles = acc.shape[0]
    bins = table_ref.shape[1] // 2
    first = first_ref[...].astype(jnp.float32)
    second = second_ref[...].astype(jnp.float32)
    even = (first + second).reshape(channels * segs, width).astype(jnp.bfloat16)
    odd = (first - second).reshape(channels * segs, width).astype(jnp.bfloat16)
    even_part = jnp.dot(even, table_ref[:, :bins], preferred_element_type=jnp.float32)
    odd_part = jnp.dot(odd, table_ref[:, bins:], preferred_element_type=jnp.float32)
    half_tiles = lane_tiles // 2

    def part_of(tile):
        part = even_part if tile < half_tiles else odd_part
        at = tile % half_tiles * 128
        return part[:, at : at + 128]

    @pl.when(step == 0)
    def _():
        for tile in range(lane_tiles):
            acc[tile] = part_of(tile)

    @pl.when(step > 0)
    def _():
        for tile in range(lane_tiles):
            acc[tile] += part_of(tile)

    @pl.when(step == pl.num_programs(0) - 1)
    def _():
        quarter = lane_tiles // 4
        reals = [*range(quarter), *range(2 * quarter, 3 * quarter)]
        for seg in range(segs):
            rows = pl.ds(seg, channels, stride=segs)
            power_sum = None
            for tile in reals:
                real, imag = acc[tile, rows, :], acc[tile + quarter, rows, :]
                power = real * real + imag * imag
                power_sum = power if power_sum is None else power_sum + power
            water = jnp.sum(power_sum, axis=1, keepdims=True) * (1.0 / bins)
            usable = valid_ref[0, seg].astype(jnp.float32)
            for place, tile in enumerate(reals):
                real, imag = acc[tile, rows, :], acc[tile + quarter, rows, :]
                power = real * real + imag * imag
                scale = lax.rsqrt(power + 0.1 * water + 1e-06) * usable
                at = place * 128
                white_ref[seg, :, at : at + 128] = (real * scale).astype(jnp.bfloat16)
                white_ref[seg, :, bins + at : bins + at + 128] = (imag * scale).astype(
                    jnp.bfloat16
                )


def whitened(records, valid_mask, table):
    channels, segs, samples = records.shape
    width = samples // 2 // STEPS
    return pl.pallas_call(
        spectra_kernel,
        name="spectra",
        grid_spec=pltpu.PrefetchScalarGridSpec(
            num_scalar_prefetch=1,
            grid=(STEPS,),
            in_specs=[
                pl.BlockSpec((channels, segs, width), lambda k, valid: (0, 0, k)),
                pl.BlockSpec((channels, segs, width), lambda k, valid: (0, 0, k + STEPS)),
                pl.BlockSpec((width, 2 * BINS), lambda k, valid: (k, 0)),
            ],
            out_specs=pl.BlockSpec((segs, channels, 2 * BINS), lambda k, valid: (0, 0, 0)),
            scratch_shapes=[
                pltpu.VMEM((2 * BINS // 128, channels * segs, 128), jnp.float32),
            ],
        ),
        out_shape=jax.ShapeDtypeStruct((segs, channels, 2 * BINS), jnp.bfloat16),
        compiler_params=pltpu.CompilerParams(vmem_limit_bytes=56 << 20),
        cost_estimate=pl.CostEstimate(
            flops=2 * channels * segs * samples * BINS,
            bytes_accessed=2 * channels * segs * samples + 2 * samples * BINS,
            transcendentals=channels * segs * BINS,
        ),
    )(valid_mask, records, records, table)


CH_TILE = 16


def cross_kernel(lowest_ref, own_ref, next_ref, far_ref, lag_ref, out_ref, wide, mixed):
    segs, channels, columns = own_ref.shape
    bins = columns // 2
    lane_tiles = bins // 128
    lowest = lowest_ref[0]
    tile = pl.program_id(0)

    @pl.when(tile == 0)
    def _():
        for hop, ref in enumerate((own_ref, next_ref, far_ref)):
            for seg in range(segs):
                for lane in range(2 * lane_tiles):
                    block = ref[seg, :, lane * 128 : lane * 128 + 128]
                    wide[seg * 2 * lane_tiles + lane, pl.ds(hop * channels, channels), :] = (
                        block.astype(jnp.float32)
                    )

    def one_channel(index, carry):
        channel = tile * CH_TILE + index
        for lane in range(lane_tiles):
            mine = []
            for seg in range(segs):
                for part in range(2):
                    slab = seg * 2 * lane_tiles + part * lane_tiles + lane
                    row = wide[slab, pl.ds(channel, 1), :]
                    mine.append(jnp.broadcast_to(row, (8, 128)))
            for pair in range(0, PAIRS, 16):
                reals, imags = [], []
                for half in range(2):
                    start = channel + lowest + pair + 8 * half
                    real = imag = None
                    for seg in range(segs):
                        slab = seg * 2 * lane_tiles + lane
                        their_real = wide[slab, pl.ds(start, 8), :]
                        their_imag = wide[slab + lane_tiles, pl.ds(start, 8), :]
                        my_real, my_imag = mine[2 * seg], mine[2 * seg + 1]
                        re = my_real * their_real + my_imag * their_imag
                        im = my_imag * their_real - my_real * their_imag
                        real = re if real is None else real + re
                        imag = im if imag is None else imag + im
                    reals.append(real)
                    imags.append(imag)
                rows = pl.ds(pl.multiple_of(index * PAIRS + pair, 16), 16)
                mixed[rows, lane * 128 : lane * 128 + 128] = jnp.concatenate(reals, axis=0).astype(
                    jnp.bfloat16
                )
                mixed[rows, bins + lane * 128 : bins + lane * 128 + 128] = jnp.concatenate(
                    imags, axis=0
                ).astype(jnp.bfloat16)
        return carry

    lax.fori_loop(0, CH_TILE, one_channel, 0)
    lagged = jnp.dot(mixed[...], lag_ref[...], preferred_element_type=jnp.float32)
    out_ref[...] = lagged.reshape(CH_TILE, PAIRS, LAGS).astype(out_ref.dtype)


def correlated(lowest, own, following, far, lag_table):
    segs, channels, columns = own.shape
    whole = pl.BlockSpec((segs, channels, columns), lambda i, low: (0, 0, 0))
    return pl.pallas_call(
        cross_kernel,
        name="cross",
        grid_spec=pltpu.PrefetchScalarGridSpec(
            num_scalar_prefetch=1,
            grid=(channels // CH_TILE,),
            in_specs=[
                whole,
                whole,
                whole,
                pl.BlockSpec(lag_table.shape, lambda i, low: (0, 0)),
            ],
            out_specs=pl.BlockSpec((CH_TILE, PAIRS, LAGS), lambda i, low: (i, 0, 0)),
            scratch_shapes=[
                pltpu.VMEM((segs * columns // 128, (REACH + 1) * channels, 128), jnp.float32),
                pltpu.VMEM((CH_TILE * PAIRS, columns), jnp.bfloat16),
            ],
        ),
        out_shape=jax.ShapeDtypeStruct((channels, PAIRS, LAGS), jnp.bfloat16),
        compiler_params=pltpu.CompilerParams(vmem_limit_bytes=56 << 20),
        cost_estimate=pl.CostEstimate(
            flops=2 * channels * PAIRS * columns * LAGS,
            bytes_accessed=6 * segs * channels * columns,
            transcendentals=0,
        ),
    )(lowest, own, following, far, lag_table)


def shards(records, valid_mask, band_limits):
    channels, segs, samples = records.shape
    blocks = lax.axis_size("chan")
    block = lax.axis_index("chan")
    white = whitened(records, valid_mask, jnp.asarray(dft_table_of(samples, BINS)))
    far = lax.ppermute(white, "chan", [(i + 2, i) for i in range(blocks - 2)])
    from_odd = lax.ppermute(white, "chan", [(i + 1, i) for i in range(0, blocks - 1, 2)])
    from_even = lax.ppermute(far, "chan", [(i - 1, i) for i in range(1, blocks, 2)])
    following = jnp.where(block % 2 == 0, from_odd, from_even)
    lowest = band_limits[0, 0]
    highest = band_limits[0, 1]
    partial = correlated(
        lowest[None], white, following, far, jnp.asarray(lag_table_of(samples, BINS, LAGS))
    )
    summed = lax.psum_scatter(partial, "tm", scatter_dimension=1, tiled=True).astype(jnp.float32)
    marks = lax.all_gather(valid_mask, ("chan", "tm"), axis=0, tiled=True)
    marks = marks.reshape(blocks, -1)
    marks = jnp.concatenate([marks, jnp.zeros((REACH, marks.shape[1]), jnp.int32)], axis=0)
    near = lax.dynamic_slice_in_dim(marks, block, REACH + 1, 0)
    counts = jnp.sum(near[:1] * near, axis=1)
    share = summed.shape[1]
    pair = lax.axis_index("tm") * share + jnp.arange(share, dtype=jnp.int32)
    partner = jnp.arange(channels, dtype=jnp.int32)[:, None] + lowest + pair[None, :]
    hop = partner // channels
    count = jnp.where(hop == 0, counts[0], jnp.where(hop == 1, counts[1], counts[2]))
    scale = 1.0 / jnp.maximum(count, 1).astype(jnp.float32)
    scale = jnp.where((lowest + pair < highest)[None, :], scale, 0.0)
    return summed * scale[..., None]


def solution(mesh):
    placed = (P("chan", "tm", None), P("chan", "tm"), P("chan", None))
    return jax.shard_map(
        shards, mesh=mesh, in_specs=placed, out_specs=P("chan", "tm", None), check_vma=False
    )
```

```python
import functools
import math

import jax
import jax.numpy as jnp
import numpy as np
from jax import lax
from jax.experimental import pallas as pl
from jax.experimental.pallas import tpu as pltpu
from jax.sharding import PartitionSpec as P

BINS = 512
LAGS = 128
PAIRS = 32
REACH = 2
STEPS = 3
CHUNKS = 2


def bin_order(bins):
    return np.concatenate([np.arange(0, bins, 2), np.arange(1, bins, 2)])


def dft_table_of(samples, bins):
    times = np.arange(samples // 2, dtype=np.int64)[:, None]
    freqs = 32 + bin_order(bins)[None, :]
    phase = (times * freqs % samples) * (2.0 * math.pi / samples)
    half = bins // 2
    real, imag = np.cos(phase), -np.sin(phase)
    parts = [real[:, :half], imag[:, :half], real[:, half:], imag[:, half:]]
    return np.concatenate(parts, axis=1).astype(jnp.bfloat16)


def lag_table_of(samples, bins, lags):
    freqs = 32 + bin_order(bins)[:, None]
    shifts = (np.arange(lags) - lags // 2 + samples) % samples
    phase = (freqs * shifts[None, :] % samples) * (2.0 * math.pi / samples)
    factor = 1.0 / math.sqrt(bins)
    return (np.concatenate([np.cos(phase), -np.sin(phase)], axis=0) * factor).astype(jnp.bfloat16)


def spectra_kernel(valid_ref, first_ref, second_ref, table_ref, *rest):
    *white_refs, acc = rest
    step = pl.program_id(0)
    channels, segs, width = first_ref.shape
    lane_tiles = acc.shape[0]
    bins = table_ref.shape[1] // 2
    first = first_ref[...].astype(jnp.float32)
    second = second_ref[...].astype(jnp.float32)
    even = (first + second).reshape(channels * segs, width).astype(jnp.bfloat16)
    odd = (first - second).reshape(channels * segs, width).astype(jnp.bfloat16)
    even_part = jnp.dot(even, table_ref[:, :bins], preferred_element_type=jnp.float32)
    odd_part = jnp.dot(odd, table_ref[:, bins:], preferred_element_type=jnp.float32)
    half_tiles = lane_tiles // 2

    def part_of(tile):
        part = even_part if tile < half_tiles else odd_part
        at = tile % half_tiles * 128
        return part[:, at : at + 128]

    @pl.when(step == 0)
    def _():
        for tile in range(lane_tiles):
            acc[tile] = part_of(tile)

    @pl.when(step > 0)
    def _():
        for tile in range(lane_tiles):
            acc[tile] += part_of(tile)

    @pl.when(step == pl.num_programs(0) - 1)
    def _():
        quarter = lane_tiles // 4
        reals = [*range(quarter), *range(2 * quarter, 3 * quarter)]
        for seg in range(segs):
            rows = pl.ds(seg, channels, stride=segs)
            power_sum = None
            for tile in reals:
                real, imag = acc[tile, rows, :], acc[tile + quarter, rows, :]
                power = real * real + imag * imag
                power_sum = power if power_sum is None else power_sum + power
            water = jnp.sum(power_sum, axis=1, keepdims=True) * (1.0 / bins)
            usable = valid_ref[0, seg].astype(jnp.float32)
            for place, tile in enumerate(reals):
                real, imag = acc[tile, rows, :], acc[tile + quarter, rows, :]
                power = real * real + imag * imag
                scale = lax.rsqrt(power + 0.1 * water + 1e-06) * usable
                at = place * 128
                group = segs // len(white_refs)
                white_ref = white_refs[seg // group].at[seg % group]
                white_ref[:, at : at + 128] = (real * scale).astype(jnp.bfloat16)
                white_ref[:, bins + at : bins + at + 128] = (imag * scale).astype(jnp.bfloat16)


def whitened(records, valid_mask, table):
    channels, segs, samples = records.shape
    width = samples // 2 // STEPS
    return pl.pallas_call(
        spectra_kernel,
        name="spectra",
        grid_spec=pltpu.PrefetchScalarGridSpec(
            num_scalar_prefetch=1,
            grid=(STEPS,),
            in_specs=[
                pl.BlockSpec((channels, segs, width), lambda k, valid: (0, 0, k)),
                pl.BlockSpec((channels, segs, width), lambda k, valid: (0, 0, k + STEPS)),
                pl.BlockSpec((width, 2 * BINS), lambda k, valid: (k, 0)),
            ],
            out_specs=[
                pl.BlockSpec((segs // CHUNKS, channels, 2 * BINS), lambda k, valid: (0, 0, 0))
            ]
            * CHUNKS,
            scratch_shapes=[
                pltpu.VMEM((2 * BINS // 128, channels * segs, 128), jnp.float32),
            ],
        ),
        out_shape=[jax.ShapeDtypeStruct((segs // CHUNKS, channels, 2 * BINS), jnp.bfloat16)]
        * CHUNKS,
        compiler_params=pltpu.CompilerParams(vmem_limit_bytes=56 << 20),
        cost_estimate=pl.CostEstimate(
            flops=2 * channels * segs * samples * BINS,
            bytes_accessed=2 * channels * segs * samples + 2 * samples * BINS,
            transcendentals=channels * segs * BINS,
        ),
    )(valid_mask, records, records, table)


CH_TILE = 16
TILES = 2


def cross_kernel(place_ref, scale_ref, own_ref, next_ref, far_ref, lag_ref, *rest, first, last):
    if not first:
        before_ref, *rest = rest
    if last:
        keep_ref, other_ref, send_ref, wide, mixed, turned = rest
    else:
        out_ref, wide, mixed = rest
    segs, channels, columns = own_ref.shape
    bins = columns // 2
    lane_tiles = bins // 128
    lowest = place_ref[0]
    step = pl.program_id(0)

    @pl.when(step == 0)
    def _():
        for hop, ref in enumerate((own_ref, next_ref, far_ref)):
            for seg in range(segs):
                for lane in range(2 * lane_tiles):
                    block = ref[seg, :, lane * 128 : lane * 128 + 128]
                    wide[seg * 2 * lane_tiles + lane, pl.ds(hop * channels, channels), :] = (
                        block.astype(jnp.float32)
                    )

    for tile in range(TILES):
        base = pl.multiple_of((step * TILES + tile) * CH_TILE, CH_TILE)
        for lane in range(lane_tiles):
            mine = {}
            for half in range(2):
                for seg in range(segs):
                    for part in range(2):
                        slab = (seg * 2 + part) * lane_tiles + lane
                        mine[half, seg, part] = wide[slab, pl.ds(base + 8 * half, 8), :]
            for pair in range(PAIRS):
                start = base + lowest + place_ref[1 + pair // 8] + pair % 8
                reals, imags = [], []
                for half in range(2):
                    real = imag = None
                    for seg in range(segs):
                        slab = seg * 2 * lane_tiles + lane
                        rows = pl.ds(start + 8 * half, 8)
                        their_real = wide[slab, rows, :]
                        their_imag = wide[slab + lane_tiles, rows, :]
                        my_real, my_imag = mine[half, seg, 0], mine[half, seg, 1]
                        re = my_real * their_real + my_imag * their_imag
                        im = my_imag * their_real - my_real * their_imag
                        real = re if real is None else real + re
                        imag = im if imag is None else imag + im
                    reals.append(real)
                    imags.append(imag)
                rows = slice(pair * CH_TILE, pair * CH_TILE + CH_TILE)
                at = lane * 128
                mixed[tile, rows, at : at + 128] = jnp.concatenate(reals, axis=0).astype(
                    jnp.bfloat16
                )
                mixed[tile, rows, bins + at : bins + at + 128] = jnp.concatenate(
                    imags, axis=0
                ).astype(jnp.bfloat16)
        lagged = jnp.dot(mixed[tile], lag_ref[...], preferred_element_type=jnp.float32)
        if not first:
            lagged += before_ref[tile]
        if not last:
            out_ref[tile] = lagged
            continue
        near = lax.broadcasted_iota(jnp.int32, (CH_TILE, LAGS), 0)
        for pair in range(PAIRS):
            offset = lowest + place_ref[1 + pair // 8] + pair % 8
            partner = near + (base + offset)
            scale = jnp.where(
                partner < channels,
                scale_ref[0],
                jnp.where(partner < 2 * channels, scale_ref[1], scale_ref[2]),
            )
            inside = jnp.where(offset < place_ref[5], 1.0, 0.0)
            rows = slice(pair * CH_TILE, pair * CH_TILE + CH_TILE)
            turned[pair // 8, pl.ds(pair % 8, CH_TILE, stride=8), :] = (
                lagged[rows] * (scale * inside)
            )
        shape = (CH_TILE, 8, LAGS)
        rows = slice(tile * CH_TILE, tile * CH_TILE + CH_TILE)
        keep_ref[rows] = turned[0].reshape(shape)
        other_ref[rows] = turned[1].reshape(shape)
        for side in range(2):
            send_ref[side, rows] = turned[2 + side].reshape(shape).astype(jnp.bfloat16)


def correlated(places, scales, own, following, far, lag_table, before=None, last=False):
    segs, channels, columns = own.shape
    whole = pl.BlockSpec((segs, channels, columns), lambda i, *_: (0, 0, 0))
    rows = TILES * CH_TILE
    raw = pl.BlockSpec((TILES, PAIRS * CH_TILE, LAGS), lambda i, *_: (i, 0, 0))
    raw_shape = jax.ShapeDtypeStruct((channels // CH_TILE, PAIRS * CH_TILE, LAGS), jnp.float32)
    scratch = [
        pltpu.VMEM((segs * columns // 128, (REACH + 1) * channels, 128), jnp.float32),
        pltpu.VMEM((TILES, CH_TILE * PAIRS, columns), jnp.bfloat16),
    ]
    out_specs, out_shape = raw, raw_shape
    if last:
        kept = pl.BlockSpec((rows, 8, LAGS), lambda i, *_: (i, 0, 0))
        sent = pl.BlockSpec((2, rows, 8, LAGS), lambda i, *_: (0, i, 0, 0))
        out_specs = [kept, kept, sent]
        kept_shape = jax.ShapeDtypeStruct((channels, 8, LAGS), jnp.float32)
        sent_shape = jax.ShapeDtypeStruct((2, channels, 8, LAGS), jnp.bfloat16)
        out_shape = [kept_shape, kept_shape, sent_shape]
        scratch.append(pltpu.VMEM((4, CH_TILE * 8, LAGS), jnp.float32))
    return pl.pallas_call(
        functools.partial(cross_kernel, first=before is None, last=last),
        name="cross",
        grid_spec=pltpu.PrefetchScalarGridSpec(
            num_scalar_prefetch=2,
            grid=(channels // rows,),
            in_specs=[
                whole,
                whole,
                whole,
                pl.BlockSpec(lag_table.shape, lambda i, *_: (0, 0)),
                *([] if before is None else [raw]),
            ],
            out_specs=out_specs,
            scratch_shapes=scratch,
        ),
        out_shape=out_shape,
        compiler_params=pltpu.CompilerParams(vmem_limit_bytes=56 << 20),
        cost_estimate=pl.CostEstimate(
            flops=2 * channels * PAIRS * columns * LAGS,
            bytes_accessed=6 * segs * channels * columns,
            transcendentals=0,
        ),
    )(places, scales, own, following, far, lag_table, *([] if before is None else [before]))


def shards(records, valid_mask, band_limits):
    channels, segs, samples = records.shape
    blocks = lax.axis_size("chan")
    block = lax.axis_index("chan")
    rank = lax.axis_index("tm")
    lowest = band_limits[0, 0]
    highest = band_limits[0, 1]

    hop_far = [(i + 2, i) for i in range(blocks - 2)]
    hop_near = [(i + 1, i) for i in range(blocks - 1)]
    to_even = [(i + 1, i) for i in range(0, blocks - 1, 2)]
    to_odd = [(i - 1, i) for i in range(1, blocks, 2)]
    core_swap = [(i, i ^ 1) for i in range(4)]
    side_swap = [(i, i ^ 2) for i in range(4)]

    marks = jnp.stack(
        [
            valid_mask,
            lax.ppermute(valid_mask, "chan", hop_near),
            lax.ppermute(valid_mask, "chan", hop_far),
        ]
    )
    counts = jnp.sum(marks * valid_mask[None], axis=(1, 2))
    counts += lax.ppermute(counts, "tm", core_swap)
    counts += lax.ppermute(counts, "tm", side_swap)
    scales = 1.0 / jnp.maximum(counts, 1).astype(jnp.float32)
    places = jnp.stack(
        [
            lowest,
            8 * rank,
            8 * (rank ^ 2),
            8 * (rank ^ 1),
            8 * (rank ^ 3),
            highest,
        ]
    )

    lag_table = jnp.asarray(lag_table_of(samples, BINS, LAGS))
    whites = whitened(records, valid_mask, jnp.asarray(dft_table_of(samples, BINS)))
    fars = [lax.ppermute(white, "chan", hop_far) for white in whites]
    before = None
    for at, (white, far) in enumerate(zip(whites, fars)):
        from_odd = lax.ppermute(white, "chan", to_even)
        from_even = lax.ppermute(far, "chan", to_odd)
        following = jnp.where(block % 2 == 0, from_odd, from_even)
        before = correlated(
            places, scales, white, following, far, lag_table, before, last=at == CHUNKS - 1
        )
    keep, other, send = before
    got = lax.ppermute(send, "tm", core_swap)
    passing = (other + got[1].astype(jnp.float32)).astype(jnp.bfloat16)
    passed = lax.ppermute(passing, "tm", side_swap)
    return keep + got[0].astype(jnp.float32) + passed.astype(jnp.float32)


def solution(mesh):
    placed = (P("chan", "tm", None), P("chan", "tm"), P("chan", None))
    return jax.shard_map(
        shards, mesh=mesh, in_specs=placed, out_specs=P("chan", "tm", None), check_vma=False
    )
```

```python
import functools
import math

import jax
import jax.numpy as jnp
import numpy as np
from jax import lax
from jax.experimental import pallas as pl
from jax.experimental.pallas import tpu as pltpu
from jax.sharding import PartitionSpec as P

BINS = 512
LAGS = 128
PAIRS = 32
REACH = 2
STEPS = 3


def bin_order(bins):
    return np.concatenate([np.arange(0, bins, 2), np.arange(1, bins, 2)])


def dft_table_of(samples, bins):
    times = np.arange(samples // 2, dtype=np.int64)[:, None]
    freqs = 32 + bin_order(bins)[None, :]
    phase = (times * freqs % samples) * (2.0 * math.pi / samples)
    half = bins // 2
    real, imag = np.cos(phase), -np.sin(phase)
    parts = [real[:, :half], imag[:, :half], real[:, half:], imag[:, half:]]
    return np.concatenate(parts, axis=1).astype(jnp.bfloat16)


def lag_table_of(samples, bins, lags):
    freqs = 32 + bin_order(bins)[:, None]
    shifts = (np.arange(lags) - lags // 2 + samples) % samples
    phase = (freqs * shifts[None, :] % samples) * (2.0 * math.pi / samples)
    factor = 1.0 / math.sqrt(bins)
    return (np.concatenate([np.cos(phase), -np.sin(phase)], axis=0) * factor).astype(jnp.bfloat16)


def spectra_kernel(valid_ref, first_ref, second_ref, table_ref, *rest, first_seg):
    *white_refs, acc = rest
    step = pl.program_id(0)
    channels, _, width = first_ref.shape
    lane_tiles = acc.shape[0]
    bins = table_ref.shape[1] // 2
    segs = acc.shape[1] // channels
    chosen = slice(first_seg, first_seg + segs)
    first = first_ref[:, chosen, :].astype(jnp.float32)
    second = second_ref[:, chosen, :].astype(jnp.float32)
    even = (first + second).reshape(channels * segs, width).astype(jnp.bfloat16)
    odd = (first - second).reshape(channels * segs, width).astype(jnp.bfloat16)
    even_part = jnp.dot(even, table_ref[:, :bins], preferred_element_type=jnp.float32)
    odd_part = jnp.dot(odd, table_ref[:, bins:], preferred_element_type=jnp.float32)
    half_tiles = lane_tiles // 2

    def part_of(tile):
        part = even_part if tile < half_tiles else odd_part
        at = tile % half_tiles * 128
        return part[:, at : at + 128]

    @pl.when(step == 0)
    def _():
        for tile in range(lane_tiles):
            acc[tile] = part_of(tile)

    @pl.when(step > 0)
    def _():
        for tile in range(lane_tiles):
            acc[tile] += part_of(tile)

    @pl.when(step == pl.num_programs(0) - 1)
    def _():
        quarter = lane_tiles // 4
        reals = [*range(quarter), *range(2 * quarter, 3 * quarter)]
        for seg in range(segs):
            rows = pl.ds(seg, channels, stride=segs)
            power_sum = None
            for tile in reals:
                real, imag = acc[tile, rows, :], acc[tile + quarter, rows, :]
                power = real * real + imag * imag
                power_sum = power if power_sum is None else power_sum + power
            water = jnp.sum(power_sum, axis=1, keepdims=True) * (1.0 / bins)
            usable = valid_ref[0, first_seg + seg].astype(jnp.float32)
            for place, tile in enumerate(reals):
                real, imag = acc[tile, rows, :], acc[tile + quarter, rows, :]
                power = real * real + imag * imag
                scale = lax.rsqrt(power + 0.1 * water + 1e-06) * usable
                at = place * 128
                group = segs // len(white_refs)
                white_ref = white_refs[seg // group].at[seg % group]
                white_ref[:, at : at + 128] = (real * scale).astype(jnp.bfloat16)
                white_ref[:, bins + at : bins + at + 128] = (imag * scale).astype(jnp.bfloat16)


def whitened(records, valid_mask, table, first_seg, groups, group):
    channels, segs, samples = records.shape
    width = samples // 2 // STEPS
    rows = groups * group * channels
    return pl.pallas_call(
        functools.partial(spectra_kernel, first_seg=first_seg),
        name="spectra",
        grid_spec=pltpu.PrefetchScalarGridSpec(
            num_scalar_prefetch=1,
            grid=(STEPS,),
            in_specs=[
                pl.BlockSpec((channels, segs, width), lambda k, valid: (0, 0, k)),
                pl.BlockSpec((channels, segs, width), lambda k, valid: (0, 0, k + STEPS)),
                pl.BlockSpec((width, 2 * BINS), lambda k, valid: (k, 0)),
            ],
            out_specs=[pl.BlockSpec((group, channels, 2 * BINS), lambda k, valid: (0, 0, 0))]
            * groups,
            scratch_shapes=[pltpu.VMEM((2 * BINS // 128, rows, 128), jnp.float32)],
        ),
        out_shape=[jax.ShapeDtypeStruct((group, channels, 2 * BINS), jnp.bfloat16)] * groups,
        compiler_params=pltpu.CompilerParams(vmem_limit_bytes=56 << 20),
        cost_estimate=pl.CostEstimate(
            flops=4 * rows * samples * BINS,
            bytes_accessed=2 * channels * segs * samples + 2 * samples * BINS,
            transcendentals=rows * BINS,
        ),
    )(valid_mask, records, records, table)


CH_TILE = 16
TILES = 2


def cross_kernel(place_ref, *rest, first, last):
    if last:
        scale_ref, *rest = rest
    own_ref, next_ref, far_ref, lag_ref, *rest = rest
    if not first:
        before_ref, *rest = rest
    if last:
        keep_ref, other_ref, send_ref, wide, mixed, turned = rest
    else:
        out_ref, wide, mixed = rest
    segs, channels, columns = own_ref.shape
    bins = columns // 2
    lane_tiles = bins // 128
    lowest = place_ref[0]
    step = pl.program_id(0)

    @pl.when(step == 0)
    def _():
        for hop, ref in enumerate((own_ref, next_ref, far_ref)):
            for seg in range(segs):
                for lane in range(2 * lane_tiles):
                    block = ref[seg, :, lane * 128 : lane * 128 + 128]
                    wide[seg * 2 * lane_tiles + lane, pl.ds(hop * channels, channels), :] = (
                        block.astype(jnp.float32)
                    )

    for tile in range(TILES):
        base = pl.multiple_of((step * TILES + tile) * CH_TILE, CH_TILE)
        for lane in range(lane_tiles):
            mine = {}
            for half in range(2):
                for seg in range(segs):
                    for part in range(2):
                        slab = (seg * 2 + part) * lane_tiles + lane
                        mine[half, seg, part] = wide[slab, pl.ds(base + 8 * half, 8), :]
            for pair in range(PAIRS):
                start = base + lowest + place_ref[1 + pair // 8] + pair % 8
                reals, imags = [], []
                for half in range(2):
                    real = imag = None
                    for seg in range(segs):
                        slab = seg * 2 * lane_tiles + lane
                        rows = pl.ds(start + 8 * half, 8)
                        their_real = wide[slab, rows, :]
                        their_imag = wide[slab + lane_tiles, rows, :]
                        my_real, my_imag = mine[half, seg, 0], mine[half, seg, 1]
                        re = my_real * their_real + my_imag * their_imag
                        im = my_imag * their_real - my_real * their_imag
                        real = re if real is None else real + re
                        imag = im if imag is None else imag + im
                    reals.append(real)
                    imags.append(imag)
                rows = slice(pair * CH_TILE, pair * CH_TILE + CH_TILE)
                at = lane * 128
                mixed[tile, rows, at : at + 128] = jnp.concatenate(reals, axis=0).astype(
                    jnp.bfloat16
                )
                mixed[tile, rows, bins + at : bins + at + 128] = jnp.concatenate(
                    imags, axis=0
                ).astype(jnp.bfloat16)
        lagged = jnp.dot(mixed[tile], lag_ref[...], preferred_element_type=jnp.float32)
        if not first:
            lagged += before_ref[tile]
        if not last:
            out_ref[tile] = lagged
            continue
        near = lax.broadcasted_iota(jnp.int32, (CH_TILE, LAGS), 0)
        for pair in range(PAIRS):
            offset = lowest + place_ref[1 + pair // 8] + pair % 8
            partner = near + (base + offset)
            scale = jnp.where(
                partner < channels,
                scale_ref[0],
                jnp.where(partner < 2 * channels, scale_ref[1], scale_ref[2]),
            )
            inside = jnp.where(offset < place_ref[5], 1.0, 0.0)
            rows = slice(pair * CH_TILE, pair * CH_TILE + CH_TILE)
            turned[pair // 8, pl.ds(pair % 8, CH_TILE, stride=8), :] = (
                lagged[rows] * (scale * inside)
            )
        shape = (CH_TILE, 8, LAGS)
        rows = slice(tile * CH_TILE, tile * CH_TILE + CH_TILE)
        keep_ref[rows] = turned[0].reshape(shape)
        other_ref[rows] = turned[1].reshape(shape)
        for side in range(2):
            send_ref[side, rows] = turned[2 + side].reshape(shape).astype(jnp.bfloat16)


def correlated(places, scales, own, following, far, lag_table, before=None, last=False):
    segs, channels, columns = own.shape
    whole = pl.BlockSpec((segs, channels, columns), lambda i, *_: (0, 0, 0))
    rows = TILES * CH_TILE
    raw = pl.BlockSpec((TILES, PAIRS * CH_TILE, LAGS), lambda i, *_: (i, 0, 0))
    raw_shape = jax.ShapeDtypeStruct((channels // CH_TILE, PAIRS * CH_TILE, LAGS), jnp.float32)
    scratch = [
        pltpu.VMEM((segs * columns // 128, (REACH + 1) * channels, 128), jnp.float32),
        pltpu.VMEM((TILES, CH_TILE * PAIRS, columns), jnp.bfloat16),
    ]
    out_specs, out_shape = raw, raw_shape
    if last:
        kept = pl.BlockSpec((rows, 8, LAGS), lambda i, *_: (i, 0, 0))
        sent = pl.BlockSpec((2, rows, 8, LAGS), lambda i, *_: (0, i, 0, 0))
        out_specs = [kept, kept, sent]
        kept_shape = jax.ShapeDtypeStruct((channels, 8, LAGS), jnp.float32)
        sent_shape = jax.ShapeDtypeStruct((2, channels, 8, LAGS), jnp.bfloat16)
        out_shape = [kept_shape, kept_shape, sent_shape]
        scratch.append(pltpu.VMEM((4, CH_TILE * 8, LAGS), jnp.float32))
    return pl.pallas_call(
        functools.partial(cross_kernel, first=before is None, last=last),
        name="cross",
        grid_spec=pltpu.PrefetchScalarGridSpec(
            num_scalar_prefetch=2 if last else 1,
            grid=(channels // rows,),
            in_specs=[
                whole,
                whole,
                whole,
                pl.BlockSpec(lag_table.shape, lambda i, *_: (0, 0)),
                *([] if before is None else [raw]),
            ],
            out_specs=out_specs,
            scratch_shapes=scratch,
        ),
        out_shape=out_shape,
        compiler_params=pltpu.CompilerParams(vmem_limit_bytes=56 << 20),
        cost_estimate=pl.CostEstimate(
            flops=10 * channels * PAIRS * columns * LAGS,
            bytes_accessed=6 * segs * channels * columns,
            transcendentals=0,
        ),
    )(
        places,
        *([scales] if last else []),
        own,
        following,
        far,
        lag_table,
        *([] if before is None else [before]),
    )


def shards(records, valid_mask, band_limits):
    channels, segs, samples = records.shape
    blocks = lax.axis_size("chan")
    block = lax.axis_index("chan")
    rank = lax.axis_index("tm")
    lowest = band_limits[0, 0]
    highest = band_limits[0, 1]

    hop_far = [(i + 2, i) for i in range(blocks - 2)]
    hop_near = [(i + 1, i) for i in range(blocks - 1)]
    pair_swap = [(i ^ 1, i) for i in range(blocks)]
    core_swap = [(i, i ^ 1) for i in range(4)]
    side_swap = [(i, i ^ 2) for i in range(4)]

    marks = jnp.stack(
        [
            valid_mask,
            lax.ppermute(valid_mask, "chan", hop_near),
            lax.ppermute(valid_mask, "chan", hop_far),
        ]
    )
    counts = jnp.sum(marks * valid_mask[None], axis=(1, 2))
    counts += lax.ppermute(counts, "tm", core_swap)
    counts += lax.ppermute(counts, "tm", side_swap)
    scales = 1.0 / jnp.maximum(counts, 1).astype(jnp.float32)
    places = jnp.stack(
        [
            lowest,
            8 * rank,
            8 * (rank ^ 2),
            8 * (rank ^ 1),
            8 * (rank ^ 3),
            highest,
        ]
    )

    lag_table = jnp.asarray(lag_table_of(samples, BINS, LAGS))
    table = jnp.asarray(dft_table_of(samples, BINS))
    half = segs // 2
    whites = [
        *whitened(records, valid_mask, table, 0, 1, half),
        *whitened(records, valid_mask, table, half, half, 1),
    ]
    fars = [lax.ppermute(white, "chan", hop_far) for white in whites]
    before = None
    for at, (white, far) in enumerate(zip(whites, fars)):
        passed = jnp.where(block % 2 == 0, far, white)
        following = lax.ppermute(passed, "chan", pair_swap)
        before = correlated(
            places, scales, white, following, far, lag_table, before, last=at == len(whites) - 1
        )
    keep, other, send = before
    got = lax.ppermute(send, "tm", core_swap)
    passing = (other + got[1].astype(jnp.float32)).astype(jnp.bfloat16)
    passed = lax.ppermute(passing, "tm", side_swap)
    return keep + got[0].astype(jnp.float32) + passed.astype(jnp.float32)


def solution(mesh):
    placed = (P("chan", "tm", None), P("chan", "tm"), P("chan", None))
    return jax.shard_map(
        shards, mesh=mesh, in_specs=placed, out_specs=P("chan", "tm", None), check_vma=False
    )
```

```python
import functools
import math

import jax
import jax.numpy as jnp
import numpy as np
from jax import lax
from jax.experimental import pallas as pl
from jax.experimental.pallas import tpu as pltpu
from jax.sharding import PartitionSpec as P

BINS = 512
LAGS = 128
PAIRS = 32
REACH = 2
STEPS = 3


def bin_order(bins):
    return np.concatenate([np.arange(0, bins, 2), np.arange(1, bins, 2)])


def dft_table_of(samples, bins):
    times = np.arange(samples // 2, dtype=np.int64)[:, None]
    freqs = 32 + bin_order(bins)[None, :]
    phase = (times * freqs % samples) * (2.0 * math.pi / samples)
    half = bins // 2
    real, imag = np.cos(phase), -np.sin(phase)
    parts = [real[:, :half], imag[:, :half], real[:, half:], imag[:, half:]]
    return np.concatenate(parts, axis=1).astype(jnp.bfloat16)


def lag_table_of(samples, bins, lags):
    freqs = 32 + bin_order(bins)[:, None]
    shifts = (np.arange(lags) - lags // 2 + samples) % samples
    phase = (freqs * shifts[None, :] % samples) * (2.0 * math.pi / samples)
    factor = 1.0 / math.sqrt(bins)
    parts = np.stack([np.cos(phase), -np.sin(phase)]) * factor
    tiles = parts.reshape(2, bins // 128, 128, lags).transpose(1, 0, 2, 3)
    tiles = tiles.reshape(bins // 128, 256, lags)
    return np.pad(tiles, ((0, 0), (0, 0), (0, 256 - lags))).astype(jnp.bfloat16)


def spectra_kernel(valid_ref, first_ref, second_ref, table_ref, *rest, first_seg):
    *white_refs, acc = rest
    step = pl.program_id(0)
    channels, _, width = first_ref.shape
    lane_tiles = acc.shape[0]
    bins = table_ref.shape[1] // 2
    segs = acc.shape[1] // channels
    chosen = slice(first_seg, first_seg + segs)
    first = first_ref[:, chosen, :].astype(jnp.float32)
    second = second_ref[:, chosen, :].astype(jnp.float32)
    even = (first + second).reshape(channels * segs, width).astype(jnp.bfloat16)
    odd = (first - second).reshape(channels * segs, width).astype(jnp.bfloat16)
    even_part = jnp.dot(even, table_ref[:, :bins], preferred_element_type=jnp.float32)
    odd_part = jnp.dot(odd, table_ref[:, bins:], preferred_element_type=jnp.float32)
    half_tiles = lane_tiles // 2

    def part_of(tile):
        part = even_part if tile < half_tiles else odd_part
        at = tile % half_tiles * 128
        return part[:, at : at + 128]

    @pl.when(step == 0)
    def _():
        for tile in range(lane_tiles):
            acc[tile] = part_of(tile)

    @pl.when(step > 0)
    def _():
        for tile in range(lane_tiles):
            acc[tile] += part_of(tile)

    @pl.when(step == pl.num_programs(0) - 1)
    def _():
        quarter = lane_tiles // 4
        reals = [*range(quarter), *range(2 * quarter, 3 * quarter)]
        for seg in range(segs):
            rows = pl.ds(seg, channels, stride=segs)
            power_sum = None
            for tile in reals:
                real, imag = acc[tile, rows, :], acc[tile + quarter, rows, :]
                power = real * real + imag * imag
                power_sum = power if power_sum is None else power_sum + power
            water = jnp.sum(power_sum, axis=1, keepdims=True) * (1.0 / bins)
            usable = valid_ref[0, first_seg + seg].astype(jnp.float32)
            for place, tile in enumerate(reals):
                real, imag = acc[tile, rows, :], acc[tile + quarter, rows, :]
                power = real * real + imag * imag
                scale = lax.rsqrt(power + 0.1 * water + 1e-06) * usable
                at = place * 128
                group = segs // len(white_refs)
                white_ref = white_refs[seg // group].at[seg % group]
                white_ref[:, at : at + 128] = (real * scale).astype(jnp.bfloat16)
                white_ref[:, bins + at : bins + at + 128] = (imag * scale).astype(jnp.bfloat16)


def whitened(records, valid_mask, table, first_seg, groups, group):
    channels, segs, samples = records.shape
    width = samples // 2 // STEPS
    rows = groups * group * channels
    return pl.pallas_call(
        functools.partial(spectra_kernel, first_seg=first_seg),
        name="spectra",
        grid_spec=pltpu.PrefetchScalarGridSpec(
            num_scalar_prefetch=1,
            grid=(STEPS,),
            in_specs=[
                pl.BlockSpec((channels, segs, width), lambda k, valid: (0, 0, k)),
                pl.BlockSpec((channels, segs, width), lambda k, valid: (0, 0, k + STEPS)),
                pl.BlockSpec((width, 2 * BINS), lambda k, valid: (k, 0)),
            ],
            out_specs=[pl.BlockSpec((group, channels, 2 * BINS), lambda k, valid: (0, 0, 0))]
            * groups,
            scratch_shapes=[pltpu.VMEM((2 * BINS // 128, rows, 128), jnp.float32)],
        ),
        out_shape=[jax.ShapeDtypeStruct((group, channels, 2 * BINS), jnp.bfloat16)] * groups,
        compiler_params=pltpu.CompilerParams(vmem_limit_bytes=56 << 20),
        cost_estimate=pl.CostEstimate(
            flops=4 * rows * samples * BINS,
            bytes_accessed=2 * channels * segs * samples + 2 * samples * BINS,
            transcendentals=rows * BINS,
        ),
    )(valid_mask, records, records, table)


CH_TILE = 16
TILES = 2
WINDOW = 13


def cross_kernel(place_ref, *rest, specs, first, last):
    if last:
        scale_ref, *rest = rest
    own_ref, next_ref, far_ref, lag_ref, *rest = rest
    if not first:
        before_ref, *rest = rest
    if last:
        keep_ref, other_ref, send_ref, wide, turned = rest
    else:
        out_ref, wide = rest
    segs, channels, columns = own_ref.shape
    bins = columns // 2
    lane_tiles = bins // 128
    lowest = place_ref[0]
    origin = lowest // CH_TILE * CH_TILE
    step = pl.program_id(0)

    @pl.when(step == 0)
    def _():
        def one_window(index, carry):
            row = origin + index * CH_TILE
            into = pl.ds(pl.multiple_of(index * CH_TILE, CH_TILE), CH_TILE)
            for hop, ref in enumerate((own_ref, next_ref, far_ref)):

                @pl.when((row >= hop * channels) & (row < (hop + 1) * channels))
                def _():
                    rows = pl.ds(pl.multiple_of(row - hop * channels, CH_TILE), CH_TILE)
                    for seg in range(segs):
                        for lane in range(2 * lane_tiles):
                            block = ref[seg, rows, lane * 128 : lane * 128 + 128]
                            wide[seg * 2 * lane_tiles + lane, into, :] = block.astype(jnp.float32)

            return carry

        lax.fori_loop(0, WINDOW, one_window, 0)

    def all_tiles(*sums):
        for tile in range(TILES):
            one_tile(tile, sums)

    def one_tile(tile, sums):
        base = pl.multiple_of((step * TILES + tile) * CH_TILE, CH_TILE)
        for lane in range(lane_tiles):
            for unit in range(2):
                pltpu.matmul_push_rhs(lag_ref[lane], 0, unit)
            mine = {}
            for seg in range(segs):
                for part in range(2):
                    at = (part * lane_tiles + lane) * 128
                    block = own_ref[seg, pl.ds(base, CH_TILE), at : at + 128].astype(jnp.float32)
                    mine[0, seg, part], mine[1, seg, part] = block[:8], block[8:]
            for pair in range(PAIRS):
                start = base + (lowest - origin) + place_ref[1 + pair // 8] + pair % 8
                reals, imags = [], []
                for half in range(2):
                    real = imag = None
                    for seg in range(segs):
                        slab = seg * 2 * lane_tiles + lane
                        rows = pl.ds(start + 8 * half, 8)
                        their_real = wide[slab, rows, :]
                        their_imag = wide[slab + lane_tiles, rows, :]
                        my_real, my_imag = mine[half, seg, 0], mine[half, seg, 1]
                        re = my_real * their_real + my_imag * their_imag
                        im = my_imag * their_real - my_real * their_imag
                        real = re if real is None else real + re
                        imag = im if imag is None else imag + im
                    reals.append(real)
                    imags.append(imag)
                mixed = [
                    jnp.concatenate(part, axis=0).astype(jnp.bfloat16) for part in (reals, imags)
                ]
                pltpu.matmul_acc_lhs(
                    sums[pair],
                    jnp.concatenate(mixed, axis=1),
                    load_staged_rhs=0 if pair < 2 else None,
                )
        near = lax.broadcasted_iota(jnp.int32, (CH_TILE, LAGS), 0)
        for pair in range(PAIRS):
            rows = slice(pair * CH_TILE, pair * CH_TILE + CH_TILE)
            lagged = pltpu.matmul_pop(sums[pair])[:, :LAGS]
            if not first:
                lagged += before_ref[tile, rows]
            if not last:
                out_ref[tile, rows] = lagged
                continue
            offset = lowest + place_ref[1 + pair // 8] + pair % 8
            partner = near + (base + offset)
            scale = jnp.where(
                partner < channels,
                scale_ref[0],
                jnp.where(partner < 2 * channels, scale_ref[1], scale_ref[2]),
            )
            inside = jnp.where(offset < place_ref[5], 1.0, 0.0)
            turned[pair // 8, pl.ds(pair % 8, CH_TILE, stride=8), :] = lagged * (scale * inside)
        if last:
            shape = (CH_TILE, 8, LAGS)
            rows = slice(tile * CH_TILE, tile * CH_TILE + CH_TILE)
            keep_ref[rows] = turned[0].reshape(shape)
            other_ref[rows] = turned[1].reshape(shape)
            for side in range(2):
                send_ref[side, rows] = turned[2 + side].reshape(shape).astype(jnp.bfloat16)

    pl.run_scoped(all_tiles, *specs)


def correlated(mesh, places, scales, own, following, far, lag_table, before=None, last=False):
    segs, channels, columns = own.shape
    whole = pl.BlockSpec((segs, channels, columns), lambda i, *_: (0, 0, 0))
    rows = TILES * CH_TILE
    raw = pl.BlockSpec((TILES, PAIRS * CH_TILE, LAGS), lambda i, *_: (i, 0, 0))
    raw_shape = jax.ShapeDtypeStruct((channels // CH_TILE, PAIRS * CH_TILE, LAGS), jnp.float32)
    scratch = [pltpu.VMEM((segs * columns // 128, WINDOW * CH_TILE, 128), jnp.float32)]
    out_specs, out_shape = raw, raw_shape
    if last:
        kept = pl.BlockSpec((rows, 8, LAGS), lambda i, *_: (i, 0, 0))
        sent = pl.BlockSpec((2, rows, 8, LAGS), lambda i, *_: (0, i, 0, 0))
        out_specs = [kept, kept, sent]
        kept_shape = jax.ShapeDtypeStruct((channels, 8, LAGS), jnp.float32)
        sent_shape = jax.ShapeDtypeStruct((2, channels, 8, LAGS), jnp.bfloat16)
        out_shape = [kept_shape, kept_shape, sent_shape]
        scratch.append(pltpu.VMEM((4, CH_TILE * 8, LAGS), jnp.float32))
    with jax.sharding.use_abstract_mesh(mesh.abstract_mesh):
        specs = [pltpu.ACC(pair % 2)((CH_TILE, 256), jnp.float32) for pair in range(PAIRS)]
    return pl.pallas_call(
        functools.partial(cross_kernel, specs=specs, first=before is None, last=last),
        name="cross",
        grid_spec=pltpu.PrefetchScalarGridSpec(
            num_scalar_prefetch=2 if last else 1,
            grid=(channels // rows,),
            in_specs=[
                whole,
                whole,
                whole,
                pl.BlockSpec(lag_table.shape, lambda i, *_: (0, 0, 0)),
                *([] if before is None else [raw]),
            ],
            out_specs=out_specs,
            scratch_shapes=scratch,
        ),
        out_shape=out_shape,
        compiler_params=pltpu.CompilerParams(vmem_limit_bytes=56 << 20),
        cost_estimate=pl.CostEstimate(
            flops=10 * channels * PAIRS * columns * LAGS,
            bytes_accessed=6 * segs * channels * columns,
            transcendentals=0,
        ),
    )(
        places,
        *([scales] if last else []),
        own,
        following,
        far,
        lag_table,
        *([] if before is None else [before]),
    )


def shards(mesh, records, valid_mask, band_limits):
    channels, segs, samples = records.shape
    blocks = lax.axis_size("chan")
    block = lax.axis_index("chan")
    rank = lax.axis_index("tm")
    lowest = band_limits[0, 0]
    highest = band_limits[0, 1]

    hop_far = [(i + 2, i) for i in range(blocks - 2)]
    hop_near = [(i + 1, i) for i in range(blocks - 1)]
    pair_swap = [(i ^ 1, i) for i in range(blocks)]
    core_swap = [(i, i ^ 1) for i in range(4)]
    side_swap = [(i, i ^ 2) for i in range(4)]

    marks = jnp.stack(
        [
            valid_mask,
            lax.ppermute(valid_mask, "chan", hop_near),
            lax.ppermute(valid_mask, "chan", hop_far),
        ]
    )
    counts = jnp.sum(marks * valid_mask[None], axis=(1, 2))
    counts += lax.ppermute(counts, "tm", core_swap)
    counts += lax.ppermute(counts, "tm", side_swap)
    scales = 1.0 / jnp.maximum(counts, 1).astype(jnp.float32)
    places = jnp.stack(
        [
            lowest,
            8 * rank,
            8 * (rank ^ 2),
            8 * (rank ^ 1),
            8 * (rank ^ 3),
            highest,
        ]
    )

    lag_table = jnp.asarray(lag_table_of(samples, BINS, LAGS))
    table = jnp.asarray(dft_table_of(samples, BINS))
    whites = whitened(records, valid_mask, table, 0, segs, 1)
    fars = [lax.ppermute(white, "chan", hop_far) for white in whites]
    before = None
    for at, (white, far) in enumerate(zip(whites, fars)):
        passed = jnp.where(block % 2 == 0, far, white)
        following = lax.ppermute(passed, "chan", pair_swap)
        before = correlated(
            mesh, places, scales, white, following, far, lag_table, before, last=at == len(whites) - 1
        )
    keep, other, send = before
    got = lax.ppermute(send, "tm", core_swap)
    passing = (other + got[1].astype(jnp.float32)).astype(jnp.bfloat16)
    passed = lax.ppermute(passing, "tm", side_swap)
    return keep + got[0].astype(jnp.float32) + passed.astype(jnp.float32)


def solution(mesh):
    placed = (P("chan", "tm", None), P("chan", "tm"), P("chan", None))
    return jax.shard_map(
        functools.partial(shards, mesh),
        mesh=mesh,
        in_specs=placed,
        out_specs=P("chan", "tm", None),
        check_vma=False,
    )
```

```python
import functools
import math

import jax
import jax.numpy as jnp
import numpy as np
from jax import lax
from jax.experimental import pallas as pl
from jax.experimental.pallas import tpu as pltpu
from jax.sharding import PartitionSpec as P

BINS = 512
LAGS = 128
PAIRS = 32
REACH = 2
STEPS = 3


def bin_order(bins):
    return np.concatenate([np.arange(0, bins, 2), np.arange(1, bins, 2)])


def dft_table_of(samples, bins):
    times = np.arange(samples // 2, dtype=np.int64)[:, None]
    freqs = 32 + bin_order(bins)[None, :]
    phase = (times * freqs % samples) * (2.0 * math.pi / samples)
    half = bins // 2
    real, imag = np.cos(phase), -np.sin(phase)
    parts = [real[:, :half], imag[:, :half], real[:, half:], imag[:, half:]]
    return np.concatenate(parts, axis=1).astype(jnp.bfloat16)


def lag_table_of(samples, bins, lags):
    freqs = 32 + bin_order(bins)[:, None]
    shifts = (np.arange(lags) - lags // 2 + samples) % samples
    phase = (freqs * shifts[None, :] % samples) * (2.0 * math.pi / samples)
    factor = 1.0 / math.sqrt(bins)
    parts = np.stack([np.cos(phase), -np.sin(phase)]) * factor
    tiles = parts.reshape(2, bins // 128, 128, lags).transpose(1, 0, 2, 3)
    tiles = tiles.reshape(bins // 128, 256, lags)
    return np.pad(tiles, ((0, 0), (0, 0), (0, 256 - lags))).astype(jnp.bfloat16)


def spectra_kernel(valid_ref, first_ref, second_ref, table_ref, *rest, first_seg):
    *white_refs, acc = rest
    step = pl.program_id(0)
    channels, _, width = first_ref.shape
    lane_tiles = acc.shape[0]
    bins = table_ref.shape[1] // 2
    segs = acc.shape[1] // channels
    chosen = slice(first_seg, first_seg + segs)
    first = first_ref[:, chosen, :].astype(jnp.float32)
    second = second_ref[:, chosen, :].astype(jnp.float32)
    even = (first + second).reshape(channels * segs, width).astype(jnp.bfloat16)
    odd = (first - second).reshape(channels * segs, width).astype(jnp.bfloat16)
    even_part = jnp.dot(even, table_ref[:, :bins], preferred_element_type=jnp.float32)
    odd_part = jnp.dot(odd, table_ref[:, bins:], preferred_element_type=jnp.float32)
    half_tiles = lane_tiles // 2

    def part_of(tile):
        part = even_part if tile < half_tiles else odd_part
        at = tile % half_tiles * 128
        return part[:, at : at + 128]

    @pl.when(step == 0)
    def _():
        for tile in range(lane_tiles):
            acc[tile] = part_of(tile)

    @pl.when(step > 0)
    def _():
        for tile in range(lane_tiles):
            acc[tile] += part_of(tile)

    @pl.when(step == pl.num_programs(0) - 1)
    def _():
        quarter = lane_tiles // 4
        reals = [*range(quarter), *range(2 * quarter, 3 * quarter)]
        for seg in range(segs):
            rows = pl.ds(seg, channels, stride=segs)
            power_sum = None
            for tile in reals:
                real, imag = acc[tile, rows, :], acc[tile + quarter, rows, :]
                power = real * real + imag * imag
                power_sum = power if power_sum is None else power_sum + power
            water = jnp.sum(power_sum, axis=1, keepdims=True) * (1.0 / bins)
            usable = valid_ref[0, first_seg + seg].astype(jnp.float32)
            for place, tile in enumerate(reals):
                real, imag = acc[tile, rows, :], acc[tile + quarter, rows, :]
                power = real * real + imag * imag
                scale = lax.rsqrt(power + 0.1 * water + 1e-06) * usable
                at = place * 128
                group = segs // len(white_refs)
                white_ref = white_refs[seg // group].at[seg % group]
                white_ref[:, at : at + 128] = (real * scale).astype(jnp.bfloat16)
                white_ref[:, bins + at : bins + at + 128] = (imag * scale).astype(jnp.bfloat16)


def whitened(records, valid_mask, table, first_seg, groups, group):
    channels, segs, samples = records.shape
    width = samples // 2 // STEPS
    rows = groups * group * channels
    return pl.pallas_call(
        functools.partial(spectra_kernel, first_seg=first_seg),
        name="spectra",
        grid_spec=pltpu.PrefetchScalarGridSpec(
            num_scalar_prefetch=1,
            grid=(STEPS,),
            in_specs=[
                pl.BlockSpec((channels, segs, width), lambda k, valid: (0, 0, k)),
                pl.BlockSpec((channels, segs, width), lambda k, valid: (0, 0, k + STEPS)),
                pl.BlockSpec((width, 2 * BINS), lambda k, valid: (k, 0)),
            ],
            out_specs=[pl.BlockSpec((group, channels, 2 * BINS), lambda k, valid: (0, 0, 0))]
            * groups,
            scratch_shapes=[pltpu.VMEM((2 * BINS // 128, rows, 128), jnp.float32)],
        ),
        out_shape=[jax.ShapeDtypeStruct((group, channels, 2 * BINS), jnp.bfloat16)] * groups,
        compiler_params=pltpu.CompilerParams(vmem_limit_bytes=56 << 20),
        cost_estimate=pl.CostEstimate(
            flops=4 * rows * samples * BINS,
            bytes_accessed=2 * channels * segs * samples + 2 * samples * BINS,
            transcendentals=rows * BINS,
        ),
    )(valid_mask, records, records, table)


CH_TILE = 16
TILES = 2
WINDOW = 13
GROUPS = (slice(0, 2), slice(2, 4))


def cross_kernel(place_ref, *rest, segs, specs, first, last):
    if last:
        scale_ref, *rest = rest
    sources, rest = rest[: 3 * segs], rest[3 * segs :]
    lag_hbm, *rest = rest
    if not first:
        before_hbm, *rest = rest
    outs, rest = (rest[:3], rest[3:]) if last else (rest[:1], rest[1:])
    extended, lag_ref, wide, before, in_sems, out_sems, *results = rest
    if last:
        turned, *results = results
    columns = extended.shape[2]
    channels = extended.shape[1] // (REACH + 1)
    lane_tiles = columns // 256
    steps = channels // (TILES * CH_TILE)
    lowest = place_ref[0]
    origin = lowest // CH_TILE * CH_TILE

    loads = [
        pltpu.make_async_copy(
            sources[hop * segs + seg],
            extended.at[seg, pl.ds(hop * channels, channels), :],
            in_sems.at[hop * segs + seg],
        )
        for hop in range(REACH + 1)
        for seg in range(segs)
    ]
    loads.append(pltpu.make_async_copy(lag_hbm, lag_ref, in_sems.at[3 * segs]))
    if not first:
        earlier = pltpu.make_async_copy(before_hbm, before, in_sems.at[3 * segs + 1])
    for load in loads:
        load.start()
    if not first:
        earlier.start()
    for load in loads:
        load.wait()

    def one_window(index, carry):
        row = jnp.minimum(origin + index * CH_TILE, (REACH + 1) * channels - CH_TILE)
        rows = pl.ds(pl.multiple_of(row, CH_TILE), CH_TILE)
        into = pl.ds(pl.multiple_of(index * CH_TILE, CH_TILE), CH_TILE)
        for seg in range(segs):
            for lane in range(2 * lane_tiles):
                block = extended[seg, rows, lane * 128 : lane * 128 + 128]
                wide[seg * 2 * lane_tiles + lane, into, :] = block.astype(jnp.float32)
        return carry

    lax.fori_loop(0, WINDOW, one_window, 0)
    if not first:
        earlier.wait()

    def stores(step):
        rows = pl.ds(pl.multiple_of(step * TILES * CH_TILE, TILES * CH_TILE), TILES * CH_TILE)
        if last:
            picks = [(rows,), (rows,), (slice(None), rows)]
        else:
            picks = [(pl.ds(step * TILES, TILES),)]
        return [
            pltpu.make_async_copy(result.at[pick], out.at[pick], out_sems.at[step, number])
            for number, (result, out, pick) in enumerate(zip(results, outs, picks))
        ]

    def one_step(step, sums):
        bases = [
            pl.multiple_of((step * TILES + tile) * CH_TILE, CH_TILE) for tile in range(TILES)
        ]
        for lane in range(lane_tiles):
            for unit in range(2):
                pltpu.matmul_push_rhs(lag_ref[lane], 0, unit)
            mine = {}
            for tile in range(TILES):
                for seg in range(segs):
                    for part in range(2):
                        at = (part * lane_tiles + lane) * 128
                        rows = pl.ds(bases[tile], CH_TILE)
                        block = extended[seg, rows, at : at + 128].astype(jnp.float32)
                        mine[tile, 0, seg, part] = block[:8]
                        mine[tile, 1, seg, part] = block[8:]
            for pair in range(PAIRS):
                offset = (lowest - origin) + place_ref[1 + pair // 8] + pair % 8
                for tile in range(TILES):
                    reals, imags = [], []
                    for half in range(2):
                        real = imag = None
                        for seg in range(segs):
                            slab = seg * 2 * lane_tiles + lane
                            rows = pl.ds(bases[tile] + offset + 8 * half, 8)
                            their_real = wide[slab, rows, :]
                            their_imag = wide[slab + lane_tiles, rows, :]
                            my_real = mine[tile, half, seg, 0]
                            my_imag = mine[tile, half, seg, 1]
                            re = my_real * their_real + my_imag * their_imag
                            im = my_imag * their_real - my_real * their_imag
                            real = re if real is None else real + re
                            imag = im if imag is None else imag + im
                        reals.append(real)
                        imags.append(imag)
                    mixed = [
                        jnp.concatenate(part, axis=0).astype(jnp.bfloat16)
                        for part in (reals, imags)
                    ]
                    pltpu.matmul_acc_lhs(
                        sums[TILES * pair + tile],
                        jnp.concatenate(mixed, axis=1),
                        load_staged_rhs=0 if pair == 0 else None,
                    )
        for tile in range(TILES):
            finish(step * TILES + tile, bases[tile], sums[tile::TILES])
        for store in stores(step):
            store.start()

    def finish(tile, base, sums):
        near = lax.broadcasted_iota(jnp.int32, (CH_TILE, LAGS), 0)
        for pair in range(PAIRS):
            rows = slice(pair * CH_TILE, pair * CH_TILE + CH_TILE)
            lagged = pltpu.matmul_pop(sums[pair])[:, :LAGS]
            if not first:
                lagged += before[tile, rows].astype(jnp.float32)
            if not last:
                results[0][tile, rows] = lagged.astype(jnp.bfloat16)
                continue
            offset = lowest + place_ref[1 + pair // 8] + pair % 8
            partner = near + (base + offset)
            scale = jnp.where(
                partner < channels,
                scale_ref[0],
                jnp.where(partner < 2 * channels, scale_ref[1], scale_ref[2]),
            )
            inside = jnp.where(offset < place_ref[5], 1.0, 0.0)
            turned[pair // 8, pl.ds(pair % 8, CH_TILE, stride=8), :] = lagged * (scale * inside)
        if last:
            shape = (CH_TILE, 8, LAGS)
            rows = pl.ds(base, CH_TILE)
            keep_ref, other_ref, send_ref = results
            keep_ref[rows] = turned[0].reshape(shape)
            other_ref[rows] = turned[1].reshape(shape)
            for side in range(2):
                send_ref[side, rows] = turned[2 + side].reshape(shape).astype(jnp.bfloat16)

    def all_steps(*sums):
        def body(step, carry):
            one_step(step, sums)
            return carry

        lax.fori_loop(0, steps, body, 0)

    pl.run_scoped(all_steps, *specs)

    def drain(step, carry):
        for store in stores(step):
            store.wait()
        return carry

    lax.fori_loop(0, steps, drain, 0)


def correlated(mesh, places, scales, owns, nexts, fars, lag_table, before=None, last=False):
    segs = len(owns)
    channels, columns = owns[0].shape
    steps = channels // (TILES * CH_TILE)
    raw_shape = (channels // CH_TILE, PAIRS * CH_TILE, LAGS)
    if last:
        out_shape = [
            jax.ShapeDtypeStruct((channels, 8, LAGS), jnp.float32),
            jax.ShapeDtypeStruct((channels, 8, LAGS), jnp.float32),
            jax.ShapeDtypeStruct((2, channels, 8, LAGS), jnp.bfloat16),
        ]
    else:
        out_shape = [jax.ShapeDtypeStruct(raw_shape, jnp.bfloat16)]
    scratch = [
        pltpu.VMEM((segs, (REACH + 1) * channels, columns), jnp.bfloat16),
        pltpu.VMEM(lag_table.shape, lag_table.dtype),
        pltpu.VMEM((segs * columns // 128, WINDOW * CH_TILE, 128), jnp.float32),
        pltpu.VMEM((8, 128) if before is None else raw_shape, jnp.bfloat16),
        pltpu.SemaphoreType.DMA((3 * segs + 2,)),
        pltpu.SemaphoreType.DMA((steps, 3)),
        *([pltpu.VMEM((4, CH_TILE * 8, LAGS), jnp.float32)] if last else []),
        *[pltpu.VMEM(shape.shape, shape.dtype) for shape in out_shape],
    ]
    with jax.sharding.use_abstract_mesh(mesh.abstract_mesh):
        specs = [
            pltpu.ACC(tile)((CH_TILE, 256), jnp.float32)
            for _ in range(PAIRS)
            for tile in range(TILES)
        ]
    smem = pl.BlockSpec(memory_space=pltpu.SMEM)
    anywhere = pl.BlockSpec(memory_space=pltpu.HBM)
    small = [places, scales] if last else [places]
    large = [*owns, *nexts, *fars, lag_table, *([] if before is None else [before])]
    return pl.pallas_call(
        functools.partial(cross_kernel, segs=segs, specs=specs, first=before is None, last=last),
        name="cross",
        in_specs=[smem] * len(small) + [anywhere] * len(large),
        out_specs=[anywhere] * len(out_shape),
        out_shape=out_shape,
        scratch_shapes=scratch,
        compiler_params=pltpu.CompilerParams(vmem_limit_bytes=40 << 20),
        cost_estimate=pl.CostEstimate(
            flops=10 * channels * PAIRS * columns * LAGS,
            bytes_accessed=6 * segs * channels * columns,
            transcendentals=0,
        ),
    )(*small, *large)


def shards(mesh, records, valid_mask, band_limits):
    channels, segs, samples = records.shape
    blocks = lax.axis_size("chan")
    block = lax.axis_index("chan")
    rank = lax.axis_index("tm")
    lowest = band_limits[0, 0]
    highest = band_limits[0, 1]

    hop_far = [(i + 2, i) for i in range(blocks - 2)]
    hop_near = [(i + 1, i) for i in range(blocks - 1)]
    pair_swap = [(i ^ 1, i) for i in range(blocks)]
    core_swap = [(i, i ^ 1) for i in range(4)]
    side_swap = [(i, i ^ 2) for i in range(4)]

    marks = jnp.stack(
        [
            valid_mask,
            lax.ppermute(valid_mask, "chan", hop_near),
            lax.ppermute(valid_mask, "chan", hop_far),
        ]
    )
    counts = jnp.sum(marks * valid_mask[None], axis=(1, 2))
    counts += lax.ppermute(counts, "tm", core_swap)
    counts += lax.ppermute(counts, "tm", side_swap)
    scales = 1.0 / jnp.maximum(counts, 1).astype(jnp.float32)
    places = jnp.stack(
        [
            lowest,
            8 * rank,
            8 * (rank ^ 2),
            8 * (rank ^ 1),
            8 * (rank ^ 3),
            highest,
        ]
    )

    lag_table = jnp.asarray(lag_table_of(samples, BINS, LAGS))
    table = jnp.asarray(dft_table_of(samples, BINS))
    whites = [white[0] for white in whitened(records, valid_mask, table, 0, segs, 1)]
    fars = [lax.ppermute(white, "chan", hop_far) for white in whites]
    nexts = []
    for white, far in zip(whites, fars):
        passed = jnp.where(block % 2 == 0, far, white)
        nexts.append(lax.ppermute(passed, "chan", pair_swap))
    before = None
    for part in GROUPS:
        last = part.stop == segs
        found = correlated(
            mesh, places, scales, whites[part], nexts[part], fars[part], lag_table, before, last
        )
        before = found[0]
    keep, other, send = found
    got = lax.ppermute(send, "tm", core_swap)
    passing = (other + got[1].astype(jnp.float32)).astype(jnp.bfloat16)
    passed = lax.ppermute(passing, "tm", side_swap)
    return keep + got[0].astype(jnp.float32) + passed.astype(jnp.float32)


def solution(mesh):
    placed = (P("chan", "tm", None), P("chan", "tm"), P("chan", None))
    return jax.shard_map(
        functools.partial(shards, mesh),
        mesh=mesh,
        in_specs=placed,
        out_specs=P("chan", "tm", None),
        check_vma=False,
    )
```

```python
import functools
import math

import jax
import jax.numpy as jnp
import numpy as np
from jax import lax
from jax.experimental import pallas as pl
from jax.experimental.pallas import tpu as pltpu
from jax.sharding import PartitionSpec as P

BINS = 512
LAGS = 128
PAIRS = 32
REACH = 2
STEPS = 3


def bin_order(bins):
    return np.concatenate([np.arange(0, bins, 2), np.arange(1, bins, 2)])


def dft_table_of(samples, bins):
    times = np.arange(samples // 2, dtype=np.int64)[:, None]
    freqs = 32 + bin_order(bins)[None, :]
    phase = (times * freqs % samples) * (2.0 * math.pi / samples)
    half = bins // 2
    real, imag = np.cos(phase), -np.sin(phase)
    parts = [real[:, :half], imag[:, :half], real[:, half:], imag[:, half:]]
    return np.concatenate(parts, axis=1).astype(jnp.bfloat16)


def lag_table_of(samples, bins, lags):
    freqs = 32 + bin_order(bins)[:, None]
    shifts = (np.arange(lags) - lags // 2 + samples) % samples
    phase = (freqs * shifts[None, :] % samples) * (2.0 * math.pi / samples)
    factor = 1.0 / math.sqrt(bins)
    parts = np.stack([np.cos(phase), -np.sin(phase)]) * factor
    tiles = parts.reshape(2, bins // 128, 128, lags).transpose(1, 0, 2, 3)
    tiles = tiles.reshape(bins // 128, 256, lags)
    return np.pad(tiles, ((0, 0), (0, 0), (0, 256 - lags))).astype(jnp.bfloat16)


def spectra_kernel(valid_ref, first_ref, second_ref, table_ref, *rest, first_seg):
    *white_refs, acc = rest
    step = pl.program_id(0)
    channels, _, width = first_ref.shape
    lane_tiles = acc.shape[0]
    bins = table_ref.shape[1] // 2
    segs = acc.shape[1] // channels
    chosen = slice(first_seg, first_seg + segs)
    first = first_ref[:, chosen, :].astype(jnp.float32)
    second = second_ref[:, chosen, :].astype(jnp.float32)
    even = (first + second).reshape(channels * segs, width).astype(jnp.bfloat16)
    odd = (first - second).reshape(channels * segs, width).astype(jnp.bfloat16)
    even_part = jnp.dot(even, table_ref[:, :bins], preferred_element_type=jnp.float32)
    odd_part = jnp.dot(odd, table_ref[:, bins:], preferred_element_type=jnp.float32)
    half_tiles = lane_tiles // 2

    def part_of(tile):
        part = even_part if tile < half_tiles else odd_part
        at = tile % half_tiles * 128
        return part[:, at : at + 128]

    @pl.when(step == 0)
    def _():
        for tile in range(lane_tiles):
            acc[tile] = part_of(tile)

    @pl.when(step > 0)
    def _():
        for tile in range(lane_tiles):
            acc[tile] += part_of(tile)

    @pl.when(step == pl.num_programs(0) - 1)
    def _():
        quarter = lane_tiles // 4
        reals = [*range(quarter), *range(2 * quarter, 3 * quarter)]
        for seg in range(segs):
            rows = pl.ds(seg, channels, stride=segs)
            power_sum = None
            for tile in reals:
                real, imag = acc[tile, rows, :], acc[tile + quarter, rows, :]
                power = real * real + imag * imag
                power_sum = power if power_sum is None else power_sum + power
            water = jnp.sum(power_sum, axis=1, keepdims=True) * (1.0 / bins)
            usable = valid_ref[0, first_seg + seg].astype(jnp.float32)
            for place, tile in enumerate(reals):
                real, imag = acc[tile, rows, :], acc[tile + quarter, rows, :]
                power = real * real + imag * imag
                scale = lax.rsqrt(power + 0.1 * water + 1e-06) * usable
                at = place * 128
                group = segs // len(white_refs)
                white_ref = white_refs[seg // group].at[seg % group]
                white_ref[:, at : at + 128] = (real * scale).astype(jnp.bfloat16)
                white_ref[:, bins + at : bins + at + 128] = (imag * scale).astype(jnp.bfloat16)


def whitened(records, valid_mask, table, first_seg, groups, group):
    channels, segs, samples = records.shape
    width = samples // 2 // STEPS
    rows = groups * group * channels
    return pl.pallas_call(
        functools.partial(spectra_kernel, first_seg=first_seg),
        name="spectra",
        grid_spec=pltpu.PrefetchScalarGridSpec(
            num_scalar_prefetch=1,
            grid=(STEPS,),
            in_specs=[
                pl.BlockSpec((channels, segs, width), lambda k, valid: (0, 0, k)),
                pl.BlockSpec((channels, segs, width), lambda k, valid: (0, 0, k + STEPS)),
                pl.BlockSpec((width, 2 * BINS), lambda k, valid: (k, 0)),
            ],
            out_specs=[pl.BlockSpec((group, channels, 2 * BINS), lambda k, valid: (0, 0, 0))]
            * groups,
            scratch_shapes=[pltpu.VMEM((2 * BINS // 128, rows, 128), jnp.float32)],
        ),
        out_shape=[jax.ShapeDtypeStruct((group, channels, 2 * BINS), jnp.bfloat16)] * groups,
        compiler_params=pltpu.CompilerParams(vmem_limit_bytes=56 << 20),
        cost_estimate=pl.CostEstimate(
            flops=4 * rows * samples * BINS,
            bytes_accessed=2 * channels * segs * samples + 2 * samples * BINS,
            transcendentals=rows * BINS,
        ),
    )(valid_mask, records, records, table)


CH_TILE = 16
TILES = 2
WINDOW = 13


def cross_kernel(place_ref, *rest, segs, specs, quarters, first, last):
    if last:
        scale_ref, *rest = rest
    sources, rest = rest[: 3 * segs], rest[3 * segs :]
    lag_hbm, *rest = rest
    if not first:
        before_hbm, *rest = rest
    count = len(quarters) if last else 1
    outs, rest = rest[:count], rest[count:]
    extended, lag_ref, wide, before, in_sems, out_sems, *results = rest
    if last:
        turned, *results = results
    columns = extended.shape[2]
    channels = extended.shape[1] // (REACH + 1)
    lane_tiles = columns // 256
    steps = channels // (TILES * CH_TILE)
    lowest = place_ref[0]
    origin = lowest // CH_TILE * CH_TILE

    loads = [
        pltpu.make_async_copy(
            sources[hop * segs + seg],
            extended.at[seg, pl.ds(hop * channels, channels), :],
            in_sems.at[hop * segs + seg],
        )
        for hop in range(REACH + 1)
        for seg in range(segs)
    ]
    loads.append(pltpu.make_async_copy(lag_hbm, lag_ref, in_sems.at[3 * segs]))
    if not first:
        earlier = pltpu.make_async_copy(before_hbm, before, in_sems.at[3 * segs + 1])
    for load in loads:
        load.start()
    if not first:
        earlier.start()
    for load in loads:
        load.wait()

    def one_window(index, carry):
        row = jnp.minimum(origin + index * CH_TILE, (REACH + 1) * channels - CH_TILE)
        rows = pl.ds(pl.multiple_of(row, CH_TILE), CH_TILE)
        into = pl.ds(pl.multiple_of(index * CH_TILE, CH_TILE), CH_TILE)
        for seg in range(segs):
            for lane in range(2 * lane_tiles):
                block = extended[seg, rows, lane * 128 : lane * 128 + 128]
                wide[seg * 2 * lane_tiles + lane, into, :] = block.astype(jnp.float32)
        return carry

    lax.fori_loop(0, WINDOW, one_window, 0)
    if not first:
        earlier.wait()

    def stores(step):
        rows = pl.ds(pl.multiple_of(step * TILES * CH_TILE, TILES * CH_TILE), TILES * CH_TILE)
        if last:
            picks = [(rows,)] * len(results)
        else:
            picks = [(pl.ds(step * TILES, TILES),)]
        return [
            pltpu.make_async_copy(result.at[pick], out.at[pick], out_sems.at[step, number])
            for number, (result, out, pick) in enumerate(zip(results, outs, picks))
        ]

    def one_step(step, sums):
        bases = [
            pl.multiple_of((step * TILES + tile) * CH_TILE, CH_TILE) for tile in range(TILES)
        ]
        for lane in range(lane_tiles):
            for unit in range(2):
                pltpu.matmul_push_rhs(lag_ref[lane], 0, unit)
            mine = {}
            for tile in range(TILES):
                for seg in range(segs):
                    for part in range(2):
                        at = (part * lane_tiles + lane) * 128
                        rows = pl.ds(bases[tile], CH_TILE)
                        block = extended[seg, rows, at : at + 128].astype(jnp.float32)
                        mine[tile, 0, seg, part] = block[:8]
                        mine[tile, 1, seg, part] = block[8:]
            for pair in range(8 * len(quarters)):
                quarter = quarters[pair // 8]
                offset = (lowest - origin) + place_ref[1 + quarter] + pair % 8
                for tile in range(TILES):
                    reals, imags = [], []
                    for half in range(2):
                        real = imag = None
                        for seg in range(segs):
                            slab = seg * 2 * lane_tiles + lane
                            rows = pl.ds(bases[tile] + offset + 8 * half, 8)
                            their_real = wide[slab, rows, :]
                            their_imag = wide[slab + lane_tiles, rows, :]
                            my_real = mine[tile, half, seg, 0]
                            my_imag = mine[tile, half, seg, 1]
                            re = my_real * their_real + my_imag * their_imag
                            im = my_imag * their_real - my_real * their_imag
                            real = re if real is None else real + re
                            imag = im if imag is None else imag + im
                        reals.append(real)
                        imags.append(imag)
                    mixed = [
                        jnp.concatenate(part, axis=0).astype(jnp.bfloat16)
                        for part in (reals, imags)
                    ]
                    pltpu.matmul_acc_lhs(
                        sums[TILES * pair + tile],
                        jnp.concatenate(mixed, axis=1),
                        load_staged_rhs=0 if pair == 0 else None,
                    )
        for tile in range(TILES):
            finish(step * TILES + tile, bases[tile], sums[tile::TILES])
        for store in stores(step):
            store.start()

    def finish(tile, base, sums):
        near = lax.broadcasted_iota(jnp.int32, (CH_TILE, LAGS), 0)
        for pair in range(8 * len(quarters)):
            quarter = quarters[pair // 8]
            at = pair * CH_TILE
            rows = slice(at, at + CH_TILE)
            lagged = pltpu.matmul_pop(sums[pair])[:, :LAGS]
            if not first:
                lagged += before[tile, rows].astype(jnp.float32)
            if not last:
                results[0][tile, rows] = lagged.astype(jnp.bfloat16)
                continue
            offset = lowest + place_ref[1 + quarter] + pair % 8
            partner = near + (base + offset)
            scale = jnp.where(
                partner < channels,
                scale_ref[0],
                jnp.where(partner < 2 * channels, scale_ref[1], scale_ref[2]),
            )
            inside = jnp.where(offset < place_ref[5], 1.0, 0.0)
            turned[pair // 8, pl.ds(pair % 8, CH_TILE, stride=8), :] = lagged * (scale * inside)
        if last:
            shape = (CH_TILE, 8, LAGS)
            rows = pl.ds(base, CH_TILE)
            for number, result in enumerate(results):
                result[rows] = turned[number].reshape(shape).astype(result.dtype)

    def all_steps(*sums):
        def body(step, carry):
            one_step(step, sums)
            return carry

        lax.fori_loop(0, steps, body, 0)

    pl.run_scoped(all_steps, *specs)

    def drain(step, carry):
        for store in stores(step):
            store.wait()
        return carry

    lax.fori_loop(0, steps, drain, 0)


def correlated(
    mesh, places, scales, owns, nexts, fars, lag_table, before, quarters, last
):
    segs = len(owns)
    channels, columns = owns[0].shape
    steps = channels // (TILES * CH_TILE)
    raw_shape = (channels // CH_TILE, 8 * 3 * CH_TILE, LAGS)
    if last:
        out_shape = [
            jax.ShapeDtypeStruct((channels, 8, LAGS), jnp.float32 if q < 2 else jnp.bfloat16)
            for q in quarters
        ]
    else:
        out_shape = [jax.ShapeDtypeStruct(raw_shape, jnp.bfloat16)]
    scratch = [
        pltpu.VMEM((segs, (REACH + 1) * channels, columns), jnp.bfloat16),
        pltpu.VMEM(lag_table.shape, lag_table.dtype),
        pltpu.VMEM((segs * columns // 128, WINDOW * CH_TILE, 128), jnp.float32),
        pltpu.VMEM((8, 128) if before is None else raw_shape, jnp.bfloat16),
        pltpu.SemaphoreType.DMA((3 * segs + 2,)),
        pltpu.SemaphoreType.DMA((steps, 3)),
        *([pltpu.VMEM((len(quarters), CH_TILE * 8, LAGS), jnp.float32)] if last else []),
        *[pltpu.VMEM(shape.shape, shape.dtype) for shape in out_shape],
    ]
    with jax.sharding.use_abstract_mesh(mesh.abstract_mesh):
        specs = [
            pltpu.ACC(tile)((CH_TILE, 256), jnp.float32)
            for _ in range(8 * len(quarters))
            for tile in range(TILES)
        ]
    smem = pl.BlockSpec(memory_space=pltpu.SMEM)
    anywhere = pl.BlockSpec(memory_space=pltpu.HBM)
    small = [places, scales] if last else [places]
    large = [*owns, *nexts, *fars, lag_table, *([] if before is None else [before])]
    return pl.pallas_call(
        functools.partial(
            cross_kernel,
            segs=segs,
            specs=specs,
            quarters=quarters,
            first=before is None,
            last=last,
        ),
        name="cross",
        in_specs=[smem] * len(small) + [anywhere] * len(large),
        out_specs=[anywhere] * len(out_shape),
        out_shape=out_shape,
        scratch_shapes=scratch,
        compiler_params=pltpu.CompilerParams(vmem_limit_bytes=60 << 20),
        cost_estimate=pl.CostEstimate(
            flops=20 * channels * 8 * len(quarters) * columns * LAGS,
            bytes_accessed=6 * segs * channels * columns,
            transcendentals=0,
        ),
    )(*small, *large)


def shards(mesh, records, valid_mask, band_limits):
    channels, segs, samples = records.shape
    blocks = lax.axis_size("chan")
    block = lax.axis_index("chan")
    rank = lax.axis_index("tm")
    lowest = band_limits[0, 0]
    highest = band_limits[0, 1]

    hop_far = [(i + 2, i) for i in range(blocks - 2)]
    hop_near = [(i + 1, i) for i in range(blocks - 1)]
    pair_swap = [(i ^ 1, i) for i in range(blocks)]
    core_swap = [(i, i ^ 1) for i in range(4)]
    side_swap = [(i, i ^ 2) for i in range(4)]

    marks = jnp.stack(
        [
            valid_mask,
            lax.ppermute(valid_mask, "chan", hop_near),
            lax.ppermute(valid_mask, "chan", hop_far),
        ]
    )
    counts = jnp.sum(marks * valid_mask[None], axis=(1, 2))
    counts += lax.ppermute(counts, "tm", core_swap)
    counts += lax.ppermute(counts, "tm", side_swap)
    scales = 1.0 / jnp.maximum(counts, 1).astype(jnp.float32)
    places = jnp.stack(
        [
            lowest,
            8 * rank,
            8 * (rank ^ 2),
            8 * (rank ^ 1),
            8 * (rank ^ 3),
            highest,
        ]
    )

    lag_table = jnp.asarray(lag_table_of(samples, BINS, LAGS))
    table = jnp.asarray(dft_table_of(samples, BINS))
    whites = [white[0] for white in whitened(records, valid_mask, table, 0, segs, 1)]
    fars = [lax.ppermute(white, "chan", hop_far) for white in whites]
    nexts = []
    passed = None
    for white, far in zip(whites, fars):
        if passed is not None:
            far, _ = lax.optimization_barrier((far, passed))
        passed = jnp.where(block % 2 == 0, far, white)
        nexts.append(lax.ppermute(passed, "chan", pair_swap))

    def stacked(part, quarters, before=None, last=True):
        chosen = (whites[part], nexts[part], fars[part])
        return correlated(mesh, places, scales, *chosen, lag_table, before, quarters, last)

    half = segs // 2
    (before,) = stacked(slice(0, half), (1, 3, 2), last=False)
    other, send_far, send = stacked(slice(half, segs), (1, 3, 2), before)
    got_far = lax.ppermute(send_far, "tm", core_swap)
    got = lax.ppermute(send, "tm", core_swap)
    passing = (other + got_far.astype(jnp.float32)).astype(jnp.bfloat16)
    crossed = lax.ppermute(passing, "tm", side_swap)
    scales, _ = lax.optimization_barrier((scales, passing))
    (keep,) = stacked(slice(0, segs), (0,))
    return keep + got.astype(jnp.float32) + crossed.astype(jnp.float32)


def solution(mesh):
    placed = (P("chan", "tm", None), P("chan", "tm"), P("chan", None))
    return jax.shard_map(
        functools.partial(shards, mesh),
        mesh=mesh,
        in_specs=placed,
        out_specs=P("chan", "tm", None),
        check_vma=False,
    )
```

```python
import functools
import math

import jax
import jax.numpy as jnp
import numpy as np
from jax import lax
from jax.experimental import pallas as pl
from jax.experimental.pallas import tpu as pltpu
from jax.sharding import PartitionSpec as P

BINS = 512
LAGS = 128
PAIRS = 32
REACH = 2
STEPS = 5


def bin_order(bins):
    return np.concatenate([np.arange(0, bins, 2), np.arange(1, bins, 2)])


def dft_table_of(samples, bins):
    times = np.arange(samples // 2, dtype=np.int64)[:, None]
    freqs = 32 + bin_order(bins)[None, :]
    phase = (times * freqs % samples) * (2.0 * math.pi / samples)
    half = bins // 2
    real, imag = np.cos(phase), -np.sin(phase)
    parts = [real[:, :half], imag[:, :half], real[:, half:], imag[:, half:]]
    return np.concatenate(parts, axis=1).astype(jnp.bfloat16)


def lag_table_of(samples, bins, lags):
    freqs = 32 + bin_order(bins)[:, None]
    shifts = (np.arange(lags) - lags // 2 + samples) % samples
    phase = (freqs * shifts[None, :] % samples) * (2.0 * math.pi / samples)
    factor = 1.0 / math.sqrt(bins)
    parts = np.stack([np.cos(phase), -np.sin(phase)]) * factor
    tiles = parts.reshape(2, bins // 128, 128, lags).transpose(1, 0, 2, 3)
    tiles = tiles.reshape(bins // 128, 256, lags)
    return np.pad(tiles, ((0, 0), (0, 0), (0, 256 - lags))).astype(jnp.bfloat16)


def spectra_kernel(valid_ref, first_ref, second_ref, table_ref, *rest, first_seg):
    *white_refs, acc = rest
    step = pl.program_id(0)
    channels, _, width = first_ref.shape
    lane_tiles = acc.shape[0]
    bins = table_ref.shape[1] // 2
    segs = acc.shape[1] // channels
    chosen = slice(first_seg, first_seg + segs)
    first = first_ref[:, chosen, :].astype(jnp.float32)
    second = second_ref[:, chosen, :].astype(jnp.float32)
    even = (first + second).reshape(channels * segs, width).astype(jnp.bfloat16)
    odd = (first - second).reshape(channels * segs, width).astype(jnp.bfloat16)
    even_part = jnp.dot(even, table_ref[:, :bins], preferred_element_type=jnp.float32)
    odd_part = jnp.dot(odd, table_ref[:, bins:], preferred_element_type=jnp.float32)
    half_tiles = lane_tiles // 2

    def part_of(tile):
        part = even_part if tile < half_tiles else odd_part
        at = tile % half_tiles * 128
        return part[:, at : at + 128]

    @pl.when(step == 0)
    def _():
        for tile in range(lane_tiles):
            acc[tile] = part_of(tile)

    @pl.when(step > 0)
    def _():
        for tile in range(lane_tiles):
            acc[tile] += part_of(tile)

    @pl.when(step == pl.num_programs(0) - 1)
    def _():
        quarter = lane_tiles // 4
        reals = [*range(quarter), *range(2 * quarter, 3 * quarter)]
        for seg in range(segs):
            rows = pl.ds(seg, channels, stride=segs)
            power_sum = None
            for tile in reals:
                real, imag = acc[tile, rows, :], acc[tile + quarter, rows, :]
                power = real * real + imag * imag
                power_sum = power if power_sum is None else power_sum + power
            water = jnp.sum(power_sum, axis=1, keepdims=True) * (1.0 / bins)
            usable = valid_ref[0, first_seg + seg].astype(jnp.float32)
            for place, tile in enumerate(reals):
                real, imag = acc[tile, rows, :], acc[tile + quarter, rows, :]
                power = real * real + imag * imag
                scale = lax.rsqrt(power + 0.1 * water + 1e-06) * usable
                at = place * 128
                group = segs // len(white_refs)
                white_ref = white_refs[seg // group].at[seg % group]
                white_ref[:, at : at + 128] = (real * scale).astype(jnp.bfloat16)
                white_ref[:, bins + at : bins + at + 128] = (imag * scale).astype(jnp.bfloat16)


def whitened(records, valid_mask, table, first_seg, groups, group):
    channels, segs, samples = records.shape
    width = samples // 2 // STEPS
    rows = groups * group * channels
    return pl.pallas_call(
        functools.partial(spectra_kernel, first_seg=first_seg),
        name="spectra",
        grid_spec=pltpu.PrefetchScalarGridSpec(
            num_scalar_prefetch=1,
            grid=(STEPS,),
            in_specs=[
                pl.BlockSpec((channels, segs, width), lambda k, valid: (0, 0, k)),
                pl.BlockSpec((channels, segs, width), lambda k, valid: (0, 0, k + STEPS)),
                pl.BlockSpec((width, 2 * BINS), lambda k, valid: (k, 0)),
            ],
            out_specs=[pl.BlockSpec((group, channels, 2 * BINS), lambda k, valid: (0, 0, 0))]
            * groups,
            scratch_shapes=[pltpu.VMEM((2 * BINS // 128, rows, 128), jnp.float32)],
        ),
        out_shape=[jax.ShapeDtypeStruct((group, channels, 2 * BINS), jnp.bfloat16)] * groups,
        compiler_params=pltpu.CompilerParams(vmem_limit_bytes=56 << 20),
        cost_estimate=pl.CostEstimate(
            flops=4 * rows * samples * BINS,
            bytes_accessed=2 * channels * segs * samples + 2 * samples * BINS,
            transcendentals=rows * BINS,
        ),
    )(valid_mask, records, records, table)


CH_TILE = 16
TILES = 2
WINDOW = 13


def cross_kernel(place_ref, *rest, segs, parts, specs, quarters, first, last):
    if last:
        scale_ref, *rest = rest
    sources, rest = rest[: 3 * parts], rest[3 * parts :]
    lag_hbm, *rest = rest
    if not first:
        before_hbm, *rest = rest
    count = len(quarters) if last else 1
    outs, rest = rest[:count], rest[count:]
    extended, lag_ref, wide, before, in_sems, out_sems, *results = rest
    if last:
        turned, *results = results
    columns = extended.shape[2]
    channels = extended.shape[1] // (REACH + 1)
    lane_tiles = columns // 256
    steps = channels // (TILES * CH_TILE)
    lowest = place_ref[0]
    origin = lowest // CH_TILE * CH_TILE

    group = segs // parts
    loads = [
        pltpu.make_async_copy(
            sources[hop * parts + part],
            extended.at[pl.ds(part * group, group), pl.ds(hop * channels, channels), :],
            in_sems.at[hop * parts + part],
        )
        for hop in range(REACH + 1)
        for part in range(parts)
    ]
    loads.append(pltpu.make_async_copy(lag_hbm, lag_ref, in_sems.at[3 * parts]))
    if not first:
        earlier = pltpu.make_async_copy(before_hbm, before, in_sems.at[3 * parts + 1])
    for load in loads:
        load.start()
    if not first:
        earlier.start()
    for load in loads:
        load.wait()

    def one_window(index, carry):
        row = jnp.minimum(origin + index * CH_TILE, (REACH + 1) * channels - CH_TILE)
        rows = pl.ds(pl.multiple_of(row, CH_TILE), CH_TILE)
        into = pl.ds(pl.multiple_of(index * CH_TILE, CH_TILE), CH_TILE)
        for seg in range(segs):
            for lane in range(2 * lane_tiles):
                block = extended[seg, rows, lane * 128 : lane * 128 + 128]
                wide[seg * 2 * lane_tiles + lane, into, :] = block.astype(jnp.float32)
        return carry

    lax.fori_loop(0, WINDOW, one_window, 0)
    if not first:
        earlier.wait()

    def stores(step):
        rows = pl.ds(pl.multiple_of(step * TILES * CH_TILE, TILES * CH_TILE), TILES * CH_TILE)
        if last:
            picks = [(rows,)] * len(results)
        else:
            picks = [(pl.ds(step * TILES, TILES),)]
        return [
            pltpu.make_async_copy(result.at[pick], out.at[pick], out_sems.at[step, number])
            for number, (result, out, pick) in enumerate(zip(results, outs, picks))
        ]

    def one_step(step, sums):
        bases = [
            pl.multiple_of((step * TILES + tile) * CH_TILE, CH_TILE) for tile in range(TILES)
        ]
        for lane in range(lane_tiles):
            for unit in range(2):
                pltpu.matmul_push_rhs(lag_ref[lane], 0, unit)
            mine = {}
            for tile in range(TILES):
                for seg in range(segs):
                    for part in range(2):
                        at = (part * lane_tiles + lane) * 128
                        rows = pl.ds(bases[tile], CH_TILE)
                        block = extended[seg, rows, at : at + 128].astype(jnp.float32)
                        mine[tile, 0, seg, part] = block[:8]
                        mine[tile, 1, seg, part] = block[8:]
            for pair in range(8 * len(quarters)):
                quarter = quarters[pair // 8]
                offset = (lowest - origin) + place_ref[1 + quarter] + pair % 8
                for tile in range(TILES):
                    reals, imags = [], []
                    for half in range(2):
                        real = imag = None
                        for seg in range(segs):
                            slab = seg * 2 * lane_tiles + lane
                            rows = pl.ds(bases[tile] + offset + 8 * half, 8)
                            their_real = wide[slab, rows, :]
                            their_imag = wide[slab + lane_tiles, rows, :]
                            my_real = mine[tile, half, seg, 0]
                            my_imag = mine[tile, half, seg, 1]
                            re = my_real * their_real + my_imag * their_imag
                            im = my_imag * their_real - my_real * their_imag
                            real = re if real is None else real + re
                            imag = im if imag is None else imag + im
                        reals.append(real)
                        imags.append(imag)
                    mixed = [
                        jnp.concatenate(part, axis=0).astype(jnp.bfloat16)
                        for part in (reals, imags)
                    ]
                    pltpu.matmul_acc_lhs(
                        sums[TILES * pair + tile],
                        jnp.concatenate(mixed, axis=1),
                        load_staged_rhs=0 if pair == 0 else None,
                    )
        for tile in range(TILES):
            finish(step * TILES + tile, bases[tile], sums[tile::TILES])
        for store in stores(step):
            store.start()

    def finish(tile, base, sums):
        near = lax.broadcasted_iota(jnp.int32, (CH_TILE, LAGS), 0)
        for pair in range(8 * len(quarters)):
            quarter = quarters[pair // 8]
            at = pair * CH_TILE
            rows = slice(at, at + CH_TILE)
            lagged = pltpu.matmul_pop(sums[pair])[:, :LAGS]
            if not first:
                lagged += before[tile, rows].astype(jnp.float32)
            if not last:
                results[0][tile, rows] = lagged.astype(jnp.bfloat16)
                continue
            offset = lowest + place_ref[1 + quarter] + pair % 8
            partner = near + (base + offset)
            scale = jnp.where(
                partner < channels,
                scale_ref[0],
                jnp.where(partner < 2 * channels, scale_ref[1], scale_ref[2]),
            )
            inside = jnp.where(offset < place_ref[5], 1.0, 0.0)
            turned[pair // 8, pl.ds(pair % 8, CH_TILE, stride=8), :] = lagged * (scale * inside)
        if last:
            shape = (CH_TILE, 8, LAGS)
            rows = pl.ds(base, CH_TILE)
            for number, result in enumerate(results):
                result[rows] = turned[number].reshape(shape).astype(result.dtype)

    def all_steps(*sums):
        def body(step, carry):
            one_step(step, sums)
            return carry

        lax.fori_loop(0, steps, body, 0)

    pl.run_scoped(all_steps, *specs)

    def drain(step, carry):
        for store in stores(step):
            store.wait()
        return carry

    lax.fori_loop(0, steps, drain, 0)


def correlated(
    mesh, places, scales, owns, nexts, fars, lag_table, before, quarters, last
):
    group, channels, columns = owns[0].shape
    segs = group * len(owns)
    steps = channels // (TILES * CH_TILE)
    raw_shape = (channels // CH_TILE, 8 * 3 * CH_TILE, LAGS)
    if last:
        out_shape = [
            jax.ShapeDtypeStruct((channels, 8, LAGS), jnp.float32 if q < 2 else jnp.bfloat16)
            for q in quarters
        ]
    else:
        out_shape = [jax.ShapeDtypeStruct(raw_shape, jnp.bfloat16)]
    scratch = [
        pltpu.VMEM((segs, (REACH + 1) * channels, columns), jnp.bfloat16),
        pltpu.VMEM(lag_table.shape, lag_table.dtype),
        pltpu.VMEM((segs * columns // 128, WINDOW * CH_TILE, 128), jnp.float32),
        pltpu.VMEM((8, 128) if before is None else raw_shape, jnp.bfloat16),
        pltpu.SemaphoreType.DMA((3 * len(owns) + 2,)),
        pltpu.SemaphoreType.DMA((steps, 3)),
        *([pltpu.VMEM((len(quarters), CH_TILE * 8, LAGS), jnp.float32)] if last else []),
        *[pltpu.VMEM(shape.shape, shape.dtype) for shape in out_shape],
    ]
    with jax.sharding.use_abstract_mesh(mesh.abstract_mesh):
        specs = [
            pltpu.ACC(tile)((CH_TILE, 256), jnp.float32)
            for _ in range(8 * len(quarters))
            for tile in range(TILES)
        ]
    smem = pl.BlockSpec(memory_space=pltpu.SMEM)
    anywhere = pl.BlockSpec(memory_space=pltpu.HBM)
    small = [places, scales] if last else [places]
    large = [*owns, *nexts, *fars, lag_table, *([] if before is None else [before])]
    return pl.pallas_call(
        functools.partial(
            cross_kernel,
            segs=segs,
            parts=len(owns),
            specs=specs,
            quarters=quarters,
            first=before is None,
            last=last,
        ),
        name="cross",
        in_specs=[smem] * len(small) + [anywhere] * len(large),
        out_specs=[anywhere] * len(out_shape),
        out_shape=out_shape,
        scratch_shapes=scratch,
        compiler_params=pltpu.CompilerParams(vmem_limit_bytes=60 << 20),
        cost_estimate=pl.CostEstimate(
            flops=20 * channels * 8 * len(quarters) * columns * LAGS,
            bytes_accessed=6 * segs * channels * columns,
            transcendentals=0,
        ),
    )(*small, *large)


def shards(mesh, records, valid_mask, band_limits):
    channels, segs, samples = records.shape
    blocks = lax.axis_size("chan")
    block = lax.axis_index("chan")
    rank = lax.axis_index("tm")
    lowest = band_limits[0, 0]
    highest = band_limits[0, 1]

    hop_far = [(i + 2, i) for i in range(blocks - 2)]
    hop_near = [(i + 1, i) for i in range(blocks - 1)]
    pair_swap = [(i ^ 1, i) for i in range(blocks)]
    core_swap = [(i, i ^ 1) for i in range(4)]
    side_swap = [(i, i ^ 2) for i in range(4)]

    places = jnp.stack(
        [
            lowest,
            8 * rank,
            8 * (rank ^ 2),
            8 * (rank ^ 1),
            8 * (rank ^ 3),
            highest,
        ]
    )

    lag_table = jnp.asarray(lag_table_of(samples, BINS, LAGS))
    table = jnp.asarray(dft_table_of(samples, BINS))
    half = segs // 2
    whites = [whitened(records, valid_mask, table, first, 1, half)[0] for first in (0, half)]
    fars = [lax.ppermute(white, "chan", hop_far) for white in whites]
    valid_mask, _ = lax.optimization_barrier((valid_mask, whites[1]))
    marks = jnp.stack(
        [
            valid_mask,
            lax.ppermute(valid_mask, "chan", hop_near),
            lax.ppermute(valid_mask, "chan", hop_far),
        ]
    )
    counts = jnp.sum(marks * valid_mask[None], axis=(1, 2))
    counts += lax.ppermute(counts, "tm", core_swap)
    counts += lax.ppermute(counts, "tm", side_swap)
    scales = 1.0 / jnp.maximum(counts, 1).astype(jnp.float32)
    nexts = []
    for white, far in zip(whites, fars):
        passed = jnp.where(block % 2 == 0, far, white)
        nexts.append(lax.ppermute(passed, "chan", pair_swap))

    def stacked(part, quarters, before=None, last=True):
        chosen = (whites[part], nexts[part], fars[part])
        return correlated(mesh, places, scales, *chosen, lag_table, before, quarters, last)

    (before,) = stacked(slice(0, 1), (1, 3, 2), last=False)
    other, send_far, send = stacked(slice(1, 2), (1, 3, 2), before)
    got_far = lax.ppermute(send_far, "tm", core_swap)
    got = lax.ppermute(send, "tm", core_swap)
    passing = (other + got_far.astype(jnp.float32)).astype(jnp.bfloat16)
    crossed = lax.ppermute(passing, "tm", side_swap)
    scales, _ = lax.optimization_barrier((scales, passing))
    (keep,) = stacked(slice(0, 2), (0,))
    return keep + got.astype(jnp.float32) + crossed.astype(jnp.float32)


def solution(mesh):
    placed = (P("chan", "tm", None), P("chan", "tm"), P("chan", None))
    return jax.shard_map(
        functools.partial(shards, mesh),
        mesh=mesh,
        in_specs=placed,
        out_specs=P("chan", "tm", None),
        check_vma=False,
    )
```

```python
import functools
import math

import jax
import jax.numpy as jnp
import numpy as np
from jax import lax
from jax.experimental import pallas as pl
from jax.experimental.pallas import tpu as pltpu
from jax.sharding import PartitionSpec as P

BINS = 512
LAGS = 128
PAIRS = 32
REACH = 2
STEPS = 5


def bin_order(bins):
    return np.concatenate([np.arange(0, bins, 2), np.arange(1, bins, 2)])


def dft_table_of(samples, bins):
    times = np.arange(samples // 2, dtype=np.int64)[:, None]
    freqs = 32 + bin_order(bins)[None, :]
    phase = (times * freqs % samples) * (2.0 * math.pi / samples)
    half = bins // 2
    real, imag = np.cos(phase), -np.sin(phase)
    parts = [real[:, :half], imag[:, :half], real[:, half:], imag[:, half:]]
    return np.concatenate(parts, axis=1).astype(jnp.bfloat16)


def lag_table_of(samples, bins, lags):
    freqs = 32 + bin_order(bins)[:, None]
    shifts = (np.arange(lags) - lags // 2 + samples) % samples
    phase = (freqs * shifts[None, :] % samples) * (2.0 * math.pi / samples)
    factor = 1.0 / math.sqrt(bins)
    parts = np.stack([np.cos(phase), -np.sin(phase)]) * factor
    tiles = parts.reshape(2, bins // 128, 128, lags).transpose(1, 0, 2, 3)
    tiles = tiles.reshape(bins // 128, 256, lags)
    return np.pad(tiles, ((0, 0), (0, 0), (0, 256 - lags))).astype(jnp.bfloat16)


def spectra_kernel(valid_ref, first_ref, second_ref, table_ref, *rest, first_seg):
    *white_refs, acc = rest
    step = pl.program_id(0)
    channels, _, width = first_ref.shape
    lane_tiles = acc.shape[0]
    bins = table_ref.shape[1] // 2
    segs = acc.shape[1] // channels
    chosen = slice(first_seg, first_seg + segs)
    first = first_ref[:, chosen, :].astype(jnp.float32)
    second = second_ref[:, chosen, :].astype(jnp.float32)
    even = (first + second).reshape(channels * segs, width).astype(jnp.bfloat16)
    odd = (first - second).reshape(channels * segs, width).astype(jnp.bfloat16)
    even_part = jnp.dot(even, table_ref[:, :bins], preferred_element_type=jnp.float32)
    odd_part = jnp.dot(odd, table_ref[:, bins:], preferred_element_type=jnp.float32)
    half_tiles = lane_tiles // 2

    def part_of(tile):
        part = even_part if tile < half_tiles else odd_part
        at = tile % half_tiles * 128
        return part[:, at : at + 128]

    @pl.when(step == 0)
    def _():
        for tile in range(lane_tiles):
            acc[tile] = part_of(tile)

    @pl.when(step > 0)
    def _():
        for tile in range(lane_tiles):
            acc[tile] += part_of(tile)

    @pl.when(step == pl.num_programs(0) - 1)
    def _():
        quarter = lane_tiles // 4
        reals = [*range(quarter), *range(2 * quarter, 3 * quarter)]
        for seg in range(segs):
            rows = pl.ds(seg, channels, stride=segs)
            power_sum = None
            for tile in reals:
                real, imag = acc[tile, rows, :], acc[tile + quarter, rows, :]
                power = real * real + imag * imag
                power_sum = power if power_sum is None else power_sum + power
            water = jnp.sum(power_sum, axis=1, keepdims=True) * (1.0 / bins)
            usable = valid_ref[0, first_seg + seg].astype(jnp.float32)
            for place, tile in enumerate(reals):
                real, imag = acc[tile, rows, :], acc[tile + quarter, rows, :]
                power = real * real + imag * imag
                scale = lax.rsqrt(power + 0.1 * water + 1e-06) * usable
                at = place * 128
                group = segs // len(white_refs)
                white_ref = white_refs[seg // group].at[seg % group]
                white_ref[:, at : at + 128] = (real * scale).astype(jnp.bfloat16)
                white_ref[:, bins + at : bins + at + 128] = (imag * scale).astype(jnp.bfloat16)


def whitened(records, valid_mask, table, first_seg, groups, group):
    channels, segs, samples = records.shape
    width = samples // 2 // STEPS
    rows = groups * group * channels
    return pl.pallas_call(
        functools.partial(spectra_kernel, first_seg=first_seg),
        name="spectra",
        grid_spec=pltpu.PrefetchScalarGridSpec(
            num_scalar_prefetch=1,
            grid=(STEPS,),
            in_specs=[
                pl.BlockSpec((channels, segs, width), lambda k, valid: (0, 0, k)),
                pl.BlockSpec((channels, segs, width), lambda k, valid: (0, 0, k + STEPS)),
                pl.BlockSpec((width, 2 * BINS), lambda k, valid: (k, 0)),
            ],
            out_specs=[pl.BlockSpec((group, channels, 2 * BINS), lambda k, valid: (0, 0, 0))]
            * groups,
            scratch_shapes=[pltpu.VMEM((2 * BINS // 128, rows, 128), jnp.float32)],
        ),
        out_shape=[jax.ShapeDtypeStruct((group, channels, 2 * BINS), jnp.bfloat16)] * groups,
        compiler_params=pltpu.CompilerParams(vmem_limit_bytes=56 << 20),
        cost_estimate=pl.CostEstimate(
            flops=4 * rows * samples * BINS,
            bytes_accessed=2 * channels * segs * samples + 2 * samples * BINS,
            transcendentals=rows * BINS,
        ),
    )(valid_mask, records, records, table)


CH_TILE = 16
TILES = 2
WINDOW = 13


def cross_kernel(place_ref, *rest, groups, specs, quarters, first, last):
    if last:
        scale_ref, *rest = rest
    parts, segs = len(groups), sum(groups)
    sources, rest = rest[: 3 * parts], rest[3 * parts :]
    lag_hbm, *rest = rest
    if not first:
        before_hbm, *rest = rest
    count = len(quarters) if last else 1
    outs, rest = rest[:count], rest[count:]
    extended, lag_ref, wide, before, in_sems, out_sems, *results = rest
    if last:
        turned, *results = results
    columns = extended.shape[2]
    channels = extended.shape[1] // (REACH + 1)
    lane_tiles = columns // 256
    steps = channels // (TILES * CH_TILE)
    lowest = place_ref[0]
    origin = lowest // CH_TILE * CH_TILE

    loads = []
    for number, source in enumerate(sources):
        hop, part = divmod(number, parts)
        into = pl.ds(sum(groups[:part]), groups[part])
        into = extended.at[into, pl.ds(hop * channels, channels), :]
        loads.append(pltpu.make_async_copy(source, into, in_sems.at[number]))
    loads.append(pltpu.make_async_copy(lag_hbm, lag_ref, in_sems.at[3 * parts]))
    if not first:
        earlier = pltpu.make_async_copy(before_hbm, before, in_sems.at[3 * parts + 1])
    for load in loads:
        load.start()
    if not first:
        earlier.start()
    for load in loads:
        load.wait()

    def one_window(index, carry):
        row = jnp.minimum(origin + index * CH_TILE, (REACH + 1) * channels - CH_TILE)
        rows = pl.ds(pl.multiple_of(row, CH_TILE), CH_TILE)
        into = pl.ds(pl.multiple_of(index * CH_TILE, CH_TILE), CH_TILE)
        for seg in range(segs):
            for lane in range(2 * lane_tiles):
                block = extended[seg, rows, lane * 128 : lane * 128 + 128]
                wide[seg * 2 * lane_tiles + lane, into, :] = block.astype(jnp.float32)
        return carry

    lax.fori_loop(0, WINDOW, one_window, 0)
    if not first:
        earlier.wait()

    def stores(step):
        rows = pl.ds(pl.multiple_of(step * TILES * CH_TILE, TILES * CH_TILE), TILES * CH_TILE)
        if last:
            picks = [(rows,)] * len(results)
        else:
            picks = [(pl.ds(step * TILES, TILES),)]
        return [
            pltpu.make_async_copy(result.at[pick], out.at[pick], out_sems.at[step, number])
            for number, (result, out, pick) in enumerate(zip(results, outs, picks))
        ]

    def one_step(step, sums):
        bases = [
            pl.multiple_of((step * TILES + tile) * CH_TILE, CH_TILE) for tile in range(TILES)
        ]
        for lane in range(lane_tiles):
            for unit in range(2):
                pltpu.matmul_push_rhs(lag_ref[lane], 0, unit)
            mine = {}
            for tile in range(TILES):
                for seg in range(segs):
                    for part in range(2):
                        at = (part * lane_tiles + lane) * 128
                        rows = pl.ds(bases[tile], CH_TILE)
                        block = extended[seg, rows, at : at + 128].astype(jnp.float32)
                        mine[tile, 0, seg, part] = block[:8]
                        mine[tile, 1, seg, part] = block[8:]
            for pair in range(8 * len(quarters)):
                quarter = quarters[pair // 8]
                offset = (lowest - origin) + place_ref[1 + quarter] + pair % 8
                for tile in range(TILES):
                    reals, imags = [], []
                    for half in range(2):
                        real = imag = None
                        for seg in range(segs):
                            slab = seg * 2 * lane_tiles + lane
                            rows = pl.ds(bases[tile] + offset + 8 * half, 8)
                            their_real = wide[slab, rows, :]
                            their_imag = wide[slab + lane_tiles, rows, :]
                            my_real = mine[tile, half, seg, 0]
                            my_imag = mine[tile, half, seg, 1]
                            re = my_real * their_real + my_imag * their_imag
                            im = my_imag * their_real - my_real * their_imag
                            real = re if real is None else real + re
                            imag = im if imag is None else imag + im
                        reals.append(real)
                        imags.append(imag)
                    mixed = [
                        jnp.concatenate(part, axis=0).astype(jnp.bfloat16)
                        for part in (reals, imags)
                    ]
                    pltpu.matmul_acc_lhs(
                        sums[TILES * pair + tile],
                        jnp.concatenate(mixed, axis=1),
                        load_staged_rhs=0 if pair == 0 else None,
                    )
        for tile in range(TILES):
            finish(step * TILES + tile, bases[tile], sums[tile::TILES])
        for store in stores(step):
            store.start()

    def finish(tile, base, sums):
        near = lax.broadcasted_iota(jnp.int32, (CH_TILE, LAGS), 0)
        for pair in range(8 * len(quarters)):
            quarter = quarters[pair // 8]
            at = pair * CH_TILE
            rows = slice(at, at + CH_TILE)
            lagged = pltpu.matmul_pop(sums[pair])[:, :LAGS]
            if not first:
                lagged += before[tile, rows].astype(jnp.float32)
            if not last:
                results[0][tile, rows] = lagged.astype(jnp.bfloat16)
                continue
            offset = lowest + place_ref[1 + quarter] + pair % 8
            partner = near + (base + offset)
            scale = jnp.where(
                partner < channels,
                scale_ref[0],
                jnp.where(partner < 2 * channels, scale_ref[1], scale_ref[2]),
            )
            inside = jnp.where(offset < place_ref[5], 1.0, 0.0)
            turned[pair // 8, pl.ds(pair % 8, CH_TILE, stride=8), :] = lagged * (scale * inside)
        if last:
            shape = (CH_TILE, 8, LAGS)
            rows = pl.ds(base, CH_TILE)
            for number, result in enumerate(results):
                result[rows] = turned[number].reshape(shape).astype(result.dtype)

    def all_steps(*sums):
        def body(step, carry):
            one_step(step, sums)
            return carry

        lax.fori_loop(0, steps, body, 0)

    pl.run_scoped(all_steps, *specs)

    def drain(step, carry):
        for store in stores(step):
            store.wait()
        return carry

    lax.fori_loop(0, steps, drain, 0)


def correlated(
    mesh, places, scales, owns, nexts, fars, lag_table, before, quarters, last
):
    groups = [own.shape[0] for own in owns]
    segs = sum(groups)
    _, channels, columns = owns[0].shape
    steps = channels // (TILES * CH_TILE)
    raw_shape = (channels // CH_TILE, 8 * 3 * CH_TILE, LAGS)
    if last:
        out_shape = [
            jax.ShapeDtypeStruct((channels, 8, LAGS), jnp.float32 if q < 2 else jnp.bfloat16)
            for q in quarters
        ]
    else:
        out_shape = [jax.ShapeDtypeStruct(raw_shape, jnp.bfloat16)]
    scratch = [
        pltpu.VMEM((segs, (REACH + 1) * channels, columns), jnp.bfloat16),
        pltpu.VMEM(lag_table.shape, lag_table.dtype),
        pltpu.VMEM((segs * columns // 128, WINDOW * CH_TILE, 128), jnp.float32),
        pltpu.VMEM((8, 128) if before is None else raw_shape, jnp.bfloat16),
        pltpu.SemaphoreType.DMA((3 * len(owns) + 2,)),
        pltpu.SemaphoreType.DMA((steps, 3)),
        *([pltpu.VMEM((len(quarters), CH_TILE * 8, LAGS), jnp.float32)] if last else []),
        *[pltpu.VMEM(shape.shape, shape.dtype) for shape in out_shape],
    ]
    with jax.sharding.use_abstract_mesh(mesh.abstract_mesh):
        specs = [
            pltpu.ACC(tile)((CH_TILE, 256), jnp.float32)
            for _ in range(8 * len(quarters))
            for tile in range(TILES)
        ]
    smem = pl.BlockSpec(memory_space=pltpu.SMEM)
    anywhere = pl.BlockSpec(memory_space=pltpu.HBM)
    small = [places, scales] if last else [places]
    large = [*owns, *nexts, *fars, lag_table, *([] if before is None else [before])]
    return pl.pallas_call(
        functools.partial(
            cross_kernel,
            groups=groups,
            specs=specs,
            quarters=quarters,
            first=before is None,
            last=last,
        ),
        name="cross",
        in_specs=[smem] * len(small) + [anywhere] * len(large),
        out_specs=[anywhere] * len(out_shape),
        out_shape=out_shape,
        scratch_shapes=scratch,
        compiler_params=pltpu.CompilerParams(vmem_limit_bytes=60 << 20),
        cost_estimate=pl.CostEstimate(
            flops=20 * channels * 8 * len(quarters) * columns * LAGS,
            bytes_accessed=6 * segs * channels * columns,
            transcendentals=0,
        ),
    )(*small, *large)


def shards(mesh, records, valid_mask, band_limits):
    channels, segs, samples = records.shape
    blocks = lax.axis_size("chan")
    block = lax.axis_index("chan")
    rank = lax.axis_index("tm")
    lowest = band_limits[0, 0]
    highest = band_limits[0, 1]

    hop_far = [(i + 2, i) for i in range(blocks - 2)]
    hop_near = [(i + 1, i) for i in range(blocks - 1)]
    pair_swap = [(i ^ 1, i) for i in range(blocks)]
    core_swap = [(i, i ^ 1) for i in range(4)]
    side_swap = [(i, i ^ 2) for i in range(4)]

    places = jnp.stack(
        [
            lowest,
            8 * rank,
            8 * (rank ^ 2),
            8 * (rank ^ 1),
            8 * (rank ^ 3),
            highest,
        ]
    )

    lag_table = jnp.asarray(lag_table_of(samples, BINS, LAGS))
    table = jnp.asarray(dft_table_of(samples, BINS))
    half = segs // 2
    whites = [
        *whitened(records, valid_mask, table, 0, 1, half),
        *whitened(records, valid_mask, table, half, half, 1),
    ]
    fars = [lax.ppermute(white, "chan", hop_far) for white in whites]
    valid_mask, _ = lax.optimization_barrier((valid_mask, whites[1]))
    marks = jnp.stack(
        [
            valid_mask,
            lax.ppermute(valid_mask, "chan", hop_near),
            lax.ppermute(valid_mask, "chan", hop_far),
        ]
    )
    counts = jnp.sum(marks * valid_mask[None], axis=(1, 2))
    counts += lax.ppermute(counts, "tm", core_swap)
    counts += lax.ppermute(counts, "tm", side_swap)
    scales = 1.0 / jnp.maximum(counts, 1).astype(jnp.float32)
    nexts = []
    passed = None
    for white, far in zip(whites, fars):
        if nexts:
            far, _ = lax.optimization_barrier((far, passed))
        passed = jnp.where(block % 2 == 0, far, white)
        nexts.append(lax.ppermute(passed, "chan", pair_swap))

    def stacked(part, quarters, before=None, last=True):
        chosen = (whites[part], nexts[part], fars[part])
        return correlated(mesh, places, scales, *chosen, lag_table, before, quarters, last)

    (before,) = stacked(slice(0, 1), (1, 3, 2), last=False)
    other, send_far, send = stacked(slice(1, None), (1, 3, 2), before)
    got_far = lax.ppermute(send_far, "tm", core_swap)
    got = lax.ppermute(send, "tm", core_swap)
    passing = (other + got_far.astype(jnp.float32)).astype(jnp.bfloat16)
    crossed = lax.ppermute(passing, "tm", side_swap)
    scales, _ = lax.optimization_barrier((scales, passing))
    (keep,) = stacked(slice(None), (0,))
    return keep + got.astype(jnp.float32) + crossed.astype(jnp.float32)


def solution(mesh):
    placed = (P("chan", "tm", None), P("chan", "tm"), P("chan", None))
    return jax.shard_map(
        functools.partial(shards, mesh),
        mesh=mesh,
        in_specs=placed,
        out_specs=P("chan", "tm", None),
        check_vma=False,
    )
```

```python
import functools
import math

import jax
import jax.numpy as jnp
import numpy as np
from jax import lax
from jax.experimental import pallas as pl
from jax.experimental.pallas import tpu as pltpu
from jax.sharding import PartitionSpec as P

BINS = 512
LAGS = 128
PAIRS = 32
REACH = 2
STEPS = 5


def bin_order(bins):
    return np.concatenate([np.arange(0, bins, 2), np.arange(1, bins, 2)])


def dft_table_of(samples, bins):
    times = np.arange(samples // 2, dtype=np.int64)[:, None]
    freqs = 32 + bin_order(bins)[None, :]
    phase = (times * freqs % samples) * (2.0 * math.pi / samples)
    half = bins // 2
    real, imag = np.cos(phase), -np.sin(phase)
    parts = [real[:, :half], imag[:, :half], real[:, half:], imag[:, half:]]
    return np.concatenate(parts, axis=1).astype(jnp.bfloat16)


def lag_table_of(samples, bins, lags):
    freqs = 32 + bin_order(bins)[:, None]
    shifts = (np.arange(lags) - lags // 2 + samples) % samples
    phase = (freqs * shifts[None, :] % samples) * (2.0 * math.pi / samples)
    factor = 1.0 / math.sqrt(bins)
    parts = np.stack([np.cos(phase), -np.sin(phase)]) * factor
    tiles = parts.reshape(2, bins // 128, 128, lags).transpose(1, 0, 2, 3)
    tiles = tiles.reshape(bins // 128, 256, lags)
    return np.pad(tiles, ((0, 0), (0, 0), (0, 256 - lags))).astype(jnp.bfloat16)


def spectra_kernel(valid_ref, first_ref, second_ref, table_ref, *rest, first_seg):
    *white_refs, acc = rest
    step = pl.program_id(0)
    channels, _, width = first_ref.shape
    lane_tiles = acc.shape[0]
    bins = table_ref.shape[1] // 2
    segs = acc.shape[1] // channels
    chosen = slice(first_seg, first_seg + segs)
    first = first_ref[:, chosen, :].astype(jnp.float32)
    second = second_ref[:, chosen, :].astype(jnp.float32)
    even = (first + second).reshape(channels * segs, width).astype(jnp.bfloat16)
    odd = (first - second).reshape(channels * segs, width).astype(jnp.bfloat16)
    even_part = jnp.dot(even, table_ref[:, :bins], preferred_element_type=jnp.float32)
    odd_part = jnp.dot(odd, table_ref[:, bins:], preferred_element_type=jnp.float32)
    half_tiles = lane_tiles // 2

    def part_of(tile):
        part = even_part if tile < half_tiles else odd_part
        at = tile % half_tiles * 128
        return part[:, at : at + 128]

    @pl.when(step == 0)
    def _():
        for tile in range(lane_tiles):
            acc[tile] = part_of(tile)

    @pl.when(step > 0)
    def _():
        for tile in range(lane_tiles):
            acc[tile] += part_of(tile)

    @pl.when(step == pl.num_programs(0) - 1)
    def _():
        quarter = lane_tiles // 4
        reals = [*range(quarter), *range(2 * quarter, 3 * quarter)]
        for seg in range(segs):
            rows = pl.ds(seg, channels, stride=segs)
            power_sum = None
            for tile in reals:
                real, imag = acc[tile, rows, :], acc[tile + quarter, rows, :]
                power = real * real + imag * imag
                power_sum = power if power_sum is None else power_sum + power
            water = jnp.sum(power_sum, axis=1, keepdims=True) * (1.0 / bins)
            usable = valid_ref[0, first_seg + seg].astype(jnp.float32)
            for place, tile in enumerate(reals):
                real, imag = acc[tile, rows, :], acc[tile + quarter, rows, :]
                power = real * real + imag * imag
                scale = lax.rsqrt(power + 0.1 * water + 1e-06) * usable
                at = place * 128
                group = segs // len(white_refs)
                white_ref = white_refs[seg // group].at[seg % group]
                white_ref[:, at : at + 128] = (real * scale).astype(jnp.bfloat16)
                white_ref[:, bins + at : bins + at + 128] = (imag * scale).astype(jnp.bfloat16)


def whitened(records, valid_mask, table, first_seg, groups, group):
    channels, segs, samples = records.shape
    width = samples // 2 // STEPS
    rows = groups * group * channels
    return pl.pallas_call(
        functools.partial(spectra_kernel, first_seg=first_seg),
        name="spectra",
        grid_spec=pltpu.PrefetchScalarGridSpec(
            num_scalar_prefetch=1,
            grid=(STEPS,),
            in_specs=[
                pl.BlockSpec((channels, segs, width), lambda k, valid: (0, 0, k)),
                pl.BlockSpec((channels, segs, width), lambda k, valid: (0, 0, k + STEPS)),
                pl.BlockSpec((width, 2 * BINS), lambda k, valid: (k, 0)),
            ],
            out_specs=[pl.BlockSpec((group, channels, 2 * BINS), lambda k, valid: (0, 0, 0))]
            * groups,
            scratch_shapes=[pltpu.VMEM((2 * BINS // 128, rows, 128), jnp.float32)],
        ),
        out_shape=[jax.ShapeDtypeStruct((group, channels, 2 * BINS), jnp.bfloat16)] * groups,
        compiler_params=pltpu.CompilerParams(vmem_limit_bytes=56 << 20),
        cost_estimate=pl.CostEstimate(
            flops=4 * rows * samples * BINS,
            bytes_accessed=2 * channels * segs * samples + 2 * samples * BINS,
            transcendentals=rows * BINS,
        ),
    )(valid_mask, records, records, table)


CH_TILE = 16
TILES = 2
WINDOW = 13


def cross_kernel(place_ref, *rest, groups, specs, quarters, first, last):
    if last:
        scale_ref, *rest = rest
    parts, segs = len(groups), sum(groups)
    sources, rest = rest[: 3 * parts], rest[3 * parts :]
    lag_hbm, *rest = rest
    if not first:
        before_hbm, *rest = rest
    count = len(quarters) if last else 1
    outs, rest = rest[:count], rest[count:]
    extended, lag_ref, wide, before, in_sems, out_sems, *results = rest
    if last:
        turned, *results = results
    columns = extended.shape[2]
    channels = extended.shape[1] // (REACH + 1)
    lane_tiles = columns // 256
    steps = channels // (TILES * CH_TILE)
    lowest = place_ref[0]
    origin = lowest // CH_TILE * CH_TILE

    loads = []
    for number, source in enumerate(sources):
        hop, part = divmod(number, parts)
        into = pl.ds(sum(groups[:part]), groups[part])
        into = extended.at[into, pl.ds(hop * channels, channels), :]
        loads.append(pltpu.make_async_copy(source, into, in_sems.at[number]))
    loads.append(pltpu.make_async_copy(lag_hbm, lag_ref, in_sems.at[3 * parts]))
    if not first:
        earlier = pltpu.make_async_copy(before_hbm, before, in_sems.at[3 * parts + 1])
    for load in loads:
        load.start()
    if not first:
        earlier.start()
    for load in loads:
        load.wait()

    def one_window(index, carry):
        row = jnp.minimum(origin + index * CH_TILE, (REACH + 1) * channels - CH_TILE)
        rows = pl.ds(pl.multiple_of(row, CH_TILE), CH_TILE)
        into = pl.ds(pl.multiple_of(index * CH_TILE, CH_TILE), CH_TILE)
        for seg in range(segs):
            for lane in range(2 * lane_tiles):
                block = extended[seg, rows, lane * 128 : lane * 128 + 128]
                wide[seg * 2 * lane_tiles + lane, into, :] = block.astype(jnp.float32)
        return carry

    lax.fori_loop(0, WINDOW, one_window, 0)
    if not first:
        earlier.wait()

    def stores(step):
        rows = pl.ds(pl.multiple_of(step * TILES * CH_TILE, TILES * CH_TILE), TILES * CH_TILE)
        if last:
            picks = [(rows,)] * len(results)
        else:
            picks = [(pl.ds(step * TILES, TILES),)]
        return [
            pltpu.make_async_copy(result.at[pick], out.at[pick], out_sems.at[step, number])
            for number, (result, out, pick) in enumerate(zip(results, outs, picks))
        ]

    def one_step(step, sums):
        bases = [
            pl.multiple_of((step * TILES + tile) * CH_TILE, CH_TILE) for tile in range(TILES)
        ]
        for lane in range(lane_tiles):
            for unit in range(2):
                pltpu.matmul_push_rhs(lag_ref[lane], 0, unit)
            mine = {}
            for tile in range(TILES):
                for seg in range(segs):
                    for part in range(2):
                        at = (part * lane_tiles + lane) * 128
                        rows = pl.ds(bases[tile], CH_TILE)
                        block = extended[seg, rows, at : at + 128].astype(jnp.float32)
                        mine[tile, 0, seg, part] = block[:8]
                        mine[tile, 1, seg, part] = block[8:]
            for pair in range(8 * len(quarters)):
                quarter = quarters[pair // 8]
                offset = (lowest - origin) + place_ref[1 + quarter] + pair % 8
                for tile in range(TILES):
                    reals, imags = [], []
                    for half in range(2):
                        real = imag = None
                        for seg in range(segs):
                            slab = seg * 2 * lane_tiles + lane
                            rows = pl.ds(bases[tile] + offset + 8 * half, 8)
                            their_real = wide[slab, rows, :]
                            their_imag = wide[slab + lane_tiles, rows, :]
                            my_real = mine[tile, half, seg, 0]
                            my_imag = mine[tile, half, seg, 1]
                            re = my_real * their_real + my_imag * their_imag
                            im = my_imag * their_real - my_real * their_imag
                            real = re if real is None else real + re
                            imag = im if imag is None else imag + im
                        reals.append(real)
                        imags.append(imag)
                    mixed = [
                        jnp.concatenate(part, axis=0).astype(jnp.bfloat16)
                        for part in (reals, imags)
                    ]
                    pltpu.matmul_acc_lhs(
                        sums[TILES * pair + tile],
                        jnp.concatenate(mixed, axis=1),
                        load_staged_rhs=0 if pair == 0 else None,
                    )
        for tile in range(TILES):
            finish(step * TILES + tile, bases[tile], sums[tile::TILES])
        for store in stores(step):
            store.start()

    def finish(tile, base, sums):
        near = lax.broadcasted_iota(jnp.int32, (CH_TILE, LAGS), 0)
        for pair in range(8 * len(quarters)):
            quarter = quarters[pair // 8]
            at = pair * CH_TILE
            rows = slice(at, at + CH_TILE)
            lagged = pltpu.matmul_pop(sums[pair])[:, :LAGS]
            if not first:
                lagged += before[tile, rows].astype(jnp.float32)
            if not last:
                results[0][tile, rows] = lagged.astype(jnp.bfloat16)
                continue
            offset = lowest + place_ref[1 + quarter] + pair % 8
            partner = near + (base + offset)
            scale = jnp.where(
                partner < channels,
                scale_ref[0],
                jnp.where(partner < 2 * channels, scale_ref[1], scale_ref[2]),
            )
            inside = jnp.where(offset < place_ref[5], 1.0, 0.0)
            turned[pair // 8, pl.ds(pair % 8, CH_TILE, stride=8), :] = lagged * (scale * inside)
        if last:
            shape = (CH_TILE, 8, LAGS)
            rows = pl.ds(base, CH_TILE)
            for number, result in enumerate(results):
                result[rows] = turned[number].reshape(shape).astype(result.dtype)

    def all_steps(*sums):
        def body(step, carry):
            one_step(step, sums)
            return carry

        lax.fori_loop(0, steps, body, 0)

    pl.run_scoped(all_steps, *specs)

    def drain(step, carry):
        for store in stores(step):
            store.wait()
        return carry

    lax.fori_loop(0, steps, drain, 0)


def correlated(
    mesh, places, scales, owns, nexts, fars, lag_table, before, quarters, last
):
    groups = [own.shape[0] for own in owns]
    segs = sum(groups)
    _, channels, columns = owns[0].shape
    steps = channels // (TILES * CH_TILE)
    raw_shape = (channels // CH_TILE, 8 * 3 * CH_TILE, LAGS)
    if last:
        out_shape = [
            jax.ShapeDtypeStruct((channels, 8, LAGS), jnp.float32 if q < 2 else jnp.bfloat16)
            for q in quarters
        ]
    else:
        out_shape = [jax.ShapeDtypeStruct(raw_shape, jnp.bfloat16)]
    scratch = [
        pltpu.VMEM((segs, (REACH + 1) * channels, columns), jnp.bfloat16),
        pltpu.VMEM(lag_table.shape, lag_table.dtype),
        pltpu.VMEM((segs * columns // 128, WINDOW * CH_TILE, 128), jnp.float32),
        pltpu.VMEM((8, 128) if before is None else raw_shape, jnp.bfloat16),
        pltpu.SemaphoreType.DMA((3 * len(owns) + 2,)),
        pltpu.SemaphoreType.DMA((steps, 3)),
        *([pltpu.VMEM((len(quarters), CH_TILE * 8, LAGS), jnp.float32)] if last else []),
        *[pltpu.VMEM(shape.shape, shape.dtype) for shape in out_shape],
    ]
    with jax.sharding.use_abstract_mesh(mesh.abstract_mesh):
        specs = [
            pltpu.ACC(tile)((CH_TILE, 256), jnp.float32)
            for _ in range(8 * len(quarters))
            for tile in range(TILES)
        ]
    smem = pl.BlockSpec(memory_space=pltpu.SMEM)
    anywhere = pl.BlockSpec(memory_space=pltpu.HBM)
    small = [places, scales] if last else [places]
    large = [*owns, *nexts, *fars, lag_table, *([] if before is None else [before])]
    return pl.pallas_call(
        functools.partial(
            cross_kernel,
            groups=groups,
            specs=specs,
            quarters=quarters,
            first=before is None,
            last=last,
        ),
        name="cross",
        in_specs=[smem] * len(small) + [anywhere] * len(large),
        out_specs=[anywhere] * len(out_shape),
        out_shape=out_shape,
        scratch_shapes=scratch,
        compiler_params=pltpu.CompilerParams(vmem_limit_bytes=60 << 20),
        cost_estimate=pl.CostEstimate(
            flops=20 * channels * 8 * len(quarters) * columns * LAGS,
            bytes_accessed=6 * segs * channels * columns,
            transcendentals=0,
        ),
    )(*small, *large)


def shards(mesh, records, valid_mask, band_limits):
    channels, segs, samples = records.shape
    blocks = lax.axis_size("chan")
    block = lax.axis_index("chan")
    rank = lax.axis_index("tm")
    lowest = band_limits[0, 0]
    highest = band_limits[0, 1]

    hop_far = [(i + 2, i) for i in range(blocks - 2)]
    hop_near = [(i + 1, i) for i in range(blocks - 1)]
    pair_swap = [(i ^ 1, i) for i in range(blocks)]
    core_swap = [(i, i ^ 1) for i in range(4)]
    side_swap = [(i, i ^ 2) for i in range(4)]

    places = jnp.stack(
        [
            lowest,
            8 * rank,
            8 * (rank ^ 2),
            8 * (rank ^ 1),
            8 * (rank ^ 3),
            highest,
        ]
    )

    lag_table = jnp.asarray(lag_table_of(samples, BINS, LAGS))
    table = jnp.asarray(dft_table_of(samples, BINS))
    half = segs // 2
    whites = [
        *whitened(records, valid_mask, table, 0, 1, half),
        *whitened(records, valid_mask, table, half, half, 1),
    ]
    fars = [lax.ppermute(white, "chan", hop_far) for white in whites]
    valid_mask, _ = lax.optimization_barrier((valid_mask, whites[1]))
    marks = jnp.stack(
        [
            valid_mask,
            lax.ppermute(valid_mask, "chan", hop_near),
            lax.ppermute(valid_mask, "chan", hop_far),
        ]
    )
    counts = jnp.sum(marks * valid_mask[None], axis=(1, 2))
    nexts = []
    for white, far in zip(whites, fars):
        if nexts:
            far, _ = lax.optimization_barrier((far, (passed, counts)))
        passed = jnp.where(block % 2 == 0, far, white)
        if not nexts:
            counts, _ = lax.optimization_barrier((counts, passed))
            counts += lax.ppermute(counts, "tm", core_swap)
            counts += lax.ppermute(counts, "tm", side_swap)
        nexts.append(lax.ppermute(passed, "chan", pair_swap))
    scales = 1.0 / jnp.maximum(counts, 1).astype(jnp.float32)

    def stacked(part, quarters, before=None, last=True):
        chosen = (whites[part], nexts[part], fars[part])
        return correlated(mesh, places, scales, *chosen, lag_table, before, quarters, last)

    (before,) = stacked(slice(0, 1), (1, 3, 2), last=False)
    other, send_far, send = stacked(slice(1, None), (1, 3, 2), before)
    got_far = lax.ppermute(send_far, "tm", core_swap)
    got = lax.ppermute(send, "tm", core_swap)
    passing = (other + got_far.astype(jnp.float32)).astype(jnp.bfloat16)
    crossed = lax.ppermute(passing, "tm", side_swap)
    scales, _ = lax.optimization_barrier((scales, passing))
    (keep,) = stacked(slice(None), (0,))
    return keep + got.astype(jnp.float32) + crossed.astype(jnp.float32)


def solution(mesh):
    placed = (P("chan", "tm", None), P("chan", "tm"), P("chan", None))
    return jax.shard_map(
        functools.partial(shards, mesh),
        mesh=mesh,
        in_specs=placed,
        out_specs=P("chan", "tm", None),
        check_vma=False,
    )
```

```python
import functools
import math

import jax
import jax.numpy as jnp
import numpy as np
from jax import lax
from jax.experimental import pallas as pl
from jax.experimental.pallas import tpu as pltpu
from jax.sharding import PartitionSpec as P

BINS = 512
LAGS = 128
PAIRS = 32
REACH = 2
STEPS = 3


def bin_order(bins):
    return np.concatenate([np.arange(0, bins, 2), np.arange(1, bins, 2)])


def dft_table_of(samples, bins):
    times = np.arange(samples // 2, dtype=np.int64)[:, None]
    freqs = 32 + bin_order(bins)[None, :]
    phase = (times * freqs % samples) * (2.0 * math.pi / samples)
    half = bins // 2
    real, imag = np.cos(phase), -np.sin(phase)
    parts = [real[:, :half], imag[:, :half], real[:, half:], imag[:, half:]]
    return np.concatenate(parts, axis=1).astype(jnp.bfloat16)


def lag_table_of(samples, bins, lags):
    freqs = 32 + bin_order(bins)[:, None]
    shifts = (np.arange(lags) - lags // 2 + samples) % samples
    phase = (freqs * shifts[None, :] % samples) * (2.0 * math.pi / samples)
    factor = 1.0 / math.sqrt(bins)
    parts = np.stack([np.cos(phase), -np.sin(phase)]) * factor
    tiles = parts.reshape(2, bins // 128, 128, lags).transpose(1, 0, 2, 3)
    tiles = tiles.reshape(bins // 128, 256, lags)
    return np.pad(tiles, ((0, 0), (0, 0), (0, 256 - lags))).astype(jnp.bfloat16)


def spectra_kernel(valid_ref, records_hbm, table_ref, *rest, first_seg):
    *white_refs, acc, buffer, sems = rest
    step = pl.program_id(0)
    steps, _, channels, _, width = buffer.shape
    lane_tiles = acc.shape[0]
    bins = table_ref.shape[1] // 2
    segs = acc.shape[1] // channels

    def loads(at):
        copies = []
        for side in range(2):
            columns = pl.ds(pl.multiple_of((at + side * steps) * width, 128), width)
            source = records_hbm.at[:, first_seg : first_seg + segs, columns]
            copies.append(
                pltpu.make_async_copy(source, buffer.at[at, side], sems.at[at, side])
            )
        return copies

    @pl.when(step == 0)
    def _():
        for load in loads(0) + loads(1):
            load.start()

    @pl.when(step + 2 < steps)
    def _():
        for load in loads(step + 2):
            load.start()

    for load in loads(step):
        load.wait()
    first = buffer[step, 0].astype(jnp.float32)
    second = buffer[step, 1].astype(jnp.float32)
    even = (first + second).reshape(channels * segs, width).astype(jnp.bfloat16)
    odd = (first - second).reshape(channels * segs, width).astype(jnp.bfloat16)
    even_part = jnp.dot(even, table_ref[:, :bins], preferred_element_type=jnp.float32)
    odd_part = jnp.dot(odd, table_ref[:, bins:], preferred_element_type=jnp.float32)
    half_tiles = lane_tiles // 2

    def part_of(tile):
        part = even_part if tile < half_tiles else odd_part
        at = tile % half_tiles * 128
        return part[:, at : at + 128]

    @pl.when(step == 0)
    def _():
        for tile in range(lane_tiles):
            acc[tile] = part_of(tile)

    @pl.when(step > 0)
    def _():
        for tile in range(lane_tiles):
            acc[tile] += part_of(tile)

    @pl.when(step == pl.num_programs(0) - 1)
    def _():
        quarter = lane_tiles // 4
        reals = [*range(quarter), *range(2 * quarter, 3 * quarter)]
        for seg in range(segs):
            rows = pl.ds(seg, channels, stride=segs)
            power_sum = None
            for tile in reals:
                real, imag = acc[tile, rows, :], acc[tile + quarter, rows, :]
                power = real * real + imag * imag
                power_sum = power if power_sum is None else power_sum + power
            water = jnp.sum(power_sum, axis=1, keepdims=True) * (1.0 / bins)
            usable = valid_ref[0, first_seg + seg].astype(jnp.float32)
            for place, tile in enumerate(reals):
                real, imag = acc[tile, rows, :], acc[tile + quarter, rows, :]
                power = real * real + imag * imag
                scale = lax.rsqrt(power + 0.1 * water + 1e-06) * usable
                at = place * 128
                group = segs // len(white_refs)
                white_ref = white_refs[seg // group].at[seg % group]
                white_ref[:, at : at + 128] = (real * scale).astype(jnp.bfloat16)
                white_ref[:, bins + at : bins + at + 128] = (imag * scale).astype(jnp.bfloat16)


def whitened(records, valid_mask, table, first_seg, groups, group):
    channels, segs, samples = records.shape
    width = samples // 2 // STEPS
    rows = groups * group * channels
    return pl.pallas_call(
        functools.partial(spectra_kernel, first_seg=first_seg),
        name="spectra",
        grid_spec=pltpu.PrefetchScalarGridSpec(
            num_scalar_prefetch=1,
            grid=(STEPS,),
            in_specs=[
                pl.BlockSpec(memory_space=pltpu.HBM),
                pl.BlockSpec((width, 2 * BINS), lambda k, valid: (k, 0)),
            ],
            out_specs=[pl.BlockSpec((group, channels, 2 * BINS), lambda k, valid: (0, 0, 0))]
            * groups,
            scratch_shapes=[
                pltpu.VMEM((2 * BINS // 128, rows, 128), jnp.float32),
                pltpu.VMEM((STEPS, 2, channels, groups * group, width), jnp.bfloat16),
                pltpu.SemaphoreType.DMA((STEPS, 2)),
            ],
        ),
        out_shape=[jax.ShapeDtypeStruct((group, channels, 2 * BINS), jnp.bfloat16)] * groups,
        compiler_params=pltpu.CompilerParams(vmem_limit_bytes=56 << 20),
        cost_estimate=pl.CostEstimate(
            flops=4 * rows * samples * BINS,
            bytes_accessed=2 * channels * segs * samples + 2 * samples * BINS,
            transcendentals=rows * BINS,
        ),
    )(valid_mask, records, table)


CH_TILE = 16
TILES = 2
WINDOW = 13


def cross_kernel(band_ref, rank_ref, *rest, groups, specs, quarters, first, last):
    if last:
        scale_ref, *rest = rest
    parts, segs = len(groups), sum(groups)
    sources, rest = rest[: 3 * parts], rest[3 * parts :]
    lag_hbm, *rest = rest
    if not first:
        before_hbm, *rest = rest
    count = len(quarters) if last else 1
    outs, rest = rest[:count], rest[count:]
    extended, lag_ref, wide, before, in_sems, out_sems, *results = rest
    if last:
        turned, *results = results
    columns = extended.shape[2]
    channels = extended.shape[1] // (REACH + 1)
    lane_tiles = columns // 256
    steps = channels // (TILES * CH_TILE)
    lowest, highest, rank = band_ref[0, 0], band_ref[0, 1], rank_ref[0]
    starts = [8 * (rank ^ flip) for flip in (0, 2, 1, 3)]
    origin = lowest // CH_TILE * CH_TILE

    loads = []
    for number, source in enumerate(sources):
        hop, part = divmod(number, parts)
        into = pl.ds(sum(groups[:part]), groups[part])
        into = extended.at[into, pl.ds(hop * channels, channels), :]
        loads.append(pltpu.make_async_copy(source, into, in_sems.at[number]))
    loads.append(pltpu.make_async_copy(lag_hbm, lag_ref, in_sems.at[3 * parts]))
    if not first:
        earlier = pltpu.make_async_copy(before_hbm, before, in_sems.at[3 * parts + 1])
    for load in loads:
        load.start()
    if not first:
        earlier.start()
    for load in loads:
        load.wait()

    def one_window(index, carry):
        row = jnp.minimum(origin + index * CH_TILE, (REACH + 1) * channels - CH_TILE)
        rows = pl.ds(pl.multiple_of(row, CH_TILE), CH_TILE)
        into = pl.ds(pl.multiple_of(index * CH_TILE, CH_TILE), CH_TILE)
        for seg in range(segs):
            for lane in range(2 * lane_tiles):
                block = extended[seg, rows, lane * 128 : lane * 128 + 128]
                wide[seg * 2 * lane_tiles + lane, into, :] = block.astype(jnp.float32)
        return carry

    lax.fori_loop(0, WINDOW, one_window, 0)
    if not first:
        earlier.wait()

    def stores(step):
        rows = pl.ds(pl.multiple_of(step * TILES * CH_TILE, TILES * CH_TILE), TILES * CH_TILE)
        if last:
            picks = [(rows,)] * len(results)
        else:
            picks = [(pl.ds(step * TILES, TILES),)]
        return [
            pltpu.make_async_copy(result.at[pick], out.at[pick], out_sems.at[step, number])
            for number, (result, out, pick) in enumerate(zip(results, outs, picks))
        ]

    def one_step(step, sums):
        bases = [
            pl.multiple_of((step * TILES + tile) * CH_TILE, CH_TILE) for tile in range(TILES)
        ]
        for lane in range(lane_tiles):
            for unit in range(2):
                pltpu.matmul_push_rhs(lag_ref[lane], 0, unit)
            mine = {}
            for tile in range(TILES):
                for seg in range(segs):
                    for part in range(2):
                        at = (part * lane_tiles + lane) * 128
                        rows = pl.ds(bases[tile], CH_TILE)
                        block = extended[seg, rows, at : at + 128].astype(jnp.float32)
                        mine[tile, 0, seg, part] = block[:8]
                        mine[tile, 1, seg, part] = block[8:]
            for pair in range(8 * len(quarters)):
                quarter = quarters[pair // 8]
                offset = (lowest - origin) + starts[quarter] + pair % 8
                for tile in range(TILES):
                    reals, imags = [], []
                    for half in range(2):
                        real = imag = None
                        for seg in range(segs):
                            slab = seg * 2 * lane_tiles + lane
                            rows = pl.ds(bases[tile] + offset + 8 * half, 8)
                            their_real = wide[slab, rows, :]
                            their_imag = wide[slab + lane_tiles, rows, :]
                            my_real = mine[tile, half, seg, 0]
                            my_imag = mine[tile, half, seg, 1]
                            re = my_real * their_real + my_imag * their_imag
                            im = my_imag * their_real - my_real * their_imag
                            real = re if real is None else real + re
                            imag = im if imag is None else imag + im
                        reals.append(real)
                        imags.append(imag)
                    mixed = [
                        jnp.concatenate(part, axis=0).astype(jnp.bfloat16)
                        for part in (reals, imags)
                    ]
                    pltpu.matmul_acc_lhs(
                        sums[TILES * pair + tile],
                        jnp.concatenate(mixed, axis=1),
                        load_staged_rhs=0 if pair == 0 else None,
                    )
        for tile in range(TILES):
            finish(step * TILES + tile, bases[tile], sums[tile::TILES])
        for store in stores(step):
            store.start()

    def finish(tile, base, sums):
        near = lax.broadcasted_iota(jnp.int32, (CH_TILE, LAGS), 0)
        for pair in range(8 * len(quarters)):
            quarter = quarters[pair // 8]
            at = pair * CH_TILE
            rows = slice(at, at + CH_TILE)
            lagged = pltpu.matmul_pop(sums[pair])[:, :LAGS]
            if not first:
                lagged += before[tile, rows].astype(jnp.float32)
            if not last:
                results[0][tile, rows] = lagged.astype(jnp.bfloat16)
                continue
            offset = lowest + starts[quarter] + pair % 8
            partner = near + (base + offset)
            scale = jnp.where(
                partner < channels,
                scale_ref[0],
                jnp.where(partner < 2 * channels, scale_ref[1], scale_ref[2]),
            )
            inside = jnp.where(offset < highest, 1.0, 0.0)
            turned[pair // 8, pl.ds(pair % 8, CH_TILE, stride=8), :] = lagged * (scale * inside)
        if last:
            shape = (CH_TILE, 8, LAGS)
            rows = pl.ds(base, CH_TILE)
            for number, result in enumerate(results):
                result[rows] = turned[number].reshape(shape).astype(result.dtype)

    def all_steps(*sums):
        def body(step, carry):
            one_step(step, sums)
            return carry

        lax.fori_loop(0, steps, body, 0)

    pl.run_scoped(all_steps, *specs)

    def drain(step, carry):
        for store in stores(step):
            store.wait()
        return carry

    lax.fori_loop(0, steps, drain, 0)


def correlated(
    mesh, places, scales, owns, nexts, fars, lag_table, before, quarters, last
):
    groups = [own.shape[0] for own in owns]
    segs = sum(groups)
    _, channels, columns = owns[0].shape
    steps = channels // (TILES * CH_TILE)
    raw_shape = (channels // CH_TILE, 8 * 3 * CH_TILE, LAGS)
    if last:
        out_shape = [
            jax.ShapeDtypeStruct((channels, 8, LAGS), jnp.float32 if q < 2 else jnp.bfloat16)
            for q in quarters
        ]
    else:
        out_shape = [jax.ShapeDtypeStruct(raw_shape, jnp.bfloat16)]
    scratch = [
        pltpu.VMEM((segs, (REACH + 1) * channels, columns), jnp.bfloat16),
        pltpu.VMEM(lag_table.shape, lag_table.dtype),
        pltpu.VMEM((segs * columns // 128, WINDOW * CH_TILE, 128), jnp.float32),
        pltpu.VMEM((8, 128) if before is None else raw_shape, jnp.bfloat16),
        pltpu.SemaphoreType.DMA((3 * len(owns) + 2,)),
        pltpu.SemaphoreType.DMA((steps, 3)),
        *([pltpu.VMEM((len(quarters), CH_TILE * 8, LAGS), jnp.float32)] if last else []),
        *[pltpu.VMEM(shape.shape, shape.dtype) for shape in out_shape],
    ]
    with jax.sharding.use_abstract_mesh(mesh.abstract_mesh):
        specs = [
            pltpu.ACC(tile)((CH_TILE, 256), jnp.float32)
            for _ in range(8 * len(quarters))
            for tile in range(TILES)
        ]
    smem = pl.BlockSpec(memory_space=pltpu.SMEM)
    anywhere = pl.BlockSpec(memory_space=pltpu.HBM)
    small = [*places, scales] if last else places
    large = [*owns, *nexts, *fars, lag_table, *([] if before is None else [before])]
    return pl.pallas_call(
        functools.partial(
            cross_kernel,
            groups=groups,
            specs=specs,
            quarters=quarters,
            first=before is None,
            last=last,
        ),
        name="cross",
        in_specs=[smem] * len(small) + [anywhere] * len(large),
        out_specs=[anywhere] * len(out_shape),
        out_shape=out_shape,
        scratch_shapes=scratch,
        compiler_params=pltpu.CompilerParams(vmem_limit_bytes=60 << 20),
        cost_estimate=pl.CostEstimate(
            flops=20 * channels * 8 * len(quarters) * columns * LAGS,
            bytes_accessed=6 * segs * channels * columns,
            transcendentals=0,
        ),
    )(*small, *large)


def shards(mesh, records, valid_mask, band_limits):
    channels, segs, samples = records.shape
    blocks = lax.axis_size("chan")
    block = lax.axis_index("chan")
    rank = lax.axis_index("tm")[None]

    hop_far = [(i + 2, i) for i in range(blocks - 2)]
    hop_near = [(i + 1, i) for i in range(blocks - 1)]
    pair_swap = [(i ^ 1, i) for i in range(blocks)]
    core_swap = [(i, i ^ 1) for i in range(4)]
    side_swap = [(i, i ^ 2) for i in range(4)]

    lag_table = jnp.asarray(lag_table_of(samples, BINS, LAGS))
    table = jnp.asarray(dft_table_of(samples, BINS))
    half = segs // 2
    whites = [
        *whitened(records, valid_mask, table, 0, 1, half),
        *whitened(records, valid_mask, table, half, half, 1),
    ]
    fars = [lax.ppermute(white, "chan", hop_far) for white in whites]
    valid_mask, _ = lax.optimization_barrier((valid_mask, whites[1]))
    marks = jnp.stack(
        [
            valid_mask,
            lax.ppermute(valid_mask, "chan", hop_near),
            lax.ppermute(valid_mask, "chan", hop_far),
        ]
    )
    counts = jnp.sum(marks * valid_mask[None], axis=(1, 2))
    nexts = []
    for white, far in zip(whites, fars):
        if nexts:
            far, _ = lax.optimization_barrier((far, (passed, counts)))
        passed = jnp.where(block % 2 == 0, far, white)
        if not nexts:
            counts, _ = lax.optimization_barrier((counts, passed))
            counts += lax.ppermute(counts, "tm", core_swap)
            counts += lax.ppermute(counts, "tm", side_swap)
        nexts.append(lax.ppermute(passed, "chan", pair_swap))
    scales = 1.0 / jnp.maximum(counts, 1).astype(jnp.float32)

    def stacked(part, quarters, before=None, last=True):
        chosen = (whites[part], nexts[part], fars[part])
        return correlated(mesh, [band_limits, rank], scales, *chosen, lag_table, before, quarters, last)

    (before,) = stacked(slice(0, 1), (1, 3, 2), last=False)
    other, send_far, send = stacked(slice(1, None), (1, 3, 2), before)
    got_far = lax.ppermute(send_far, "tm", core_swap)
    got = lax.ppermute(send, "tm", core_swap)
    passing = (other + got_far.astype(jnp.float32)).astype(jnp.bfloat16)
    crossed = lax.ppermute(passing, "tm", side_swap)
    scales, _ = lax.optimization_barrier((scales, passing))
    (keep,) = stacked(slice(None), (0,))
    return keep + got.astype(jnp.float32) + crossed.astype(jnp.float32)


def solution(mesh):
    placed = (P("chan", "tm", None), P("chan", "tm"), P("chan", None))
    return jax.shard_map(
        functools.partial(shards, mesh),
        mesh=mesh,
        in_specs=placed,
        out_specs=P("chan", "tm", None),
        check_vma=False,
    )
```

```python
import functools
import math

import jax
import jax.numpy as jnp
import numpy as np
from jax import lax
from jax.experimental import pallas as pl
from jax.experimental.pallas import tpu as pltpu
from jax.sharding import PartitionSpec as P

BINS = 512
LAGS = 128
PAIRS = 32
REACH = 2
STEPS = 3


def bin_order(bins):
    return np.concatenate([np.arange(0, bins, 2), np.arange(1, bins, 2)])


def dft_table_of(samples, bins):
    times = np.arange(samples // 2, dtype=np.int64)[:, None]
    freqs = 32 + bin_order(bins)[None, :]
    phase = (times * freqs % samples) * (2.0 * math.pi / samples)
    half = bins // 2
    real, imag = np.cos(phase), -np.sin(phase)
    parts = [real[:, :half], imag[:, :half], real[:, half:], imag[:, half:]]
    return np.concatenate(parts, axis=1).astype(jnp.bfloat16)


def lag_table_of(samples, bins, lags):
    freqs = 32 + bin_order(bins)[:, None]
    shifts = (np.arange(lags) - lags // 2 + samples) % samples
    phase = (freqs * shifts[None, :] % samples) * (2.0 * math.pi / samples)
    factor = 1.0 / math.sqrt(bins)
    parts = np.stack([np.cos(phase), -np.sin(phase)]) * factor
    tiles = parts.reshape(2, bins // 128, 128, lags).transpose(1, 0, 2, 3)
    tiles = tiles.reshape(bins // 128, 256, lags)
    return np.pad(tiles, ((0, 0), (0, 0), (0, 256 - lags))).astype(jnp.bfloat16)


def spectra_kernel(valid_ref, records_hbm, table_ref, *rest, first_seg):
    *white_refs, acc, buffer, sems = rest
    step = pl.program_id(0)
    steps, _, channels, _, width = buffer.shape
    lane_tiles = acc.shape[0]
    bins = table_ref.shape[1] // 2
    segs = acc.shape[1] // channels

    def loads(at):
        copies = []
        for side in range(2):
            columns = pl.ds(pl.multiple_of((at + side * steps) * width, 128), width)
            source = records_hbm.at[:, first_seg : first_seg + segs, columns]
            copies.append(
                pltpu.make_async_copy(source, buffer.at[at, side], sems.at[at, side])
            )
        return copies

    @pl.when(step == 0)
    def _():
        for load in loads(0) + loads(1):
            load.start()

    @pl.when(step + 2 < steps)
    def _():
        for load in loads(step + 2):
            load.start()

    for load in loads(step):
        load.wait()
    first = buffer[step, 0].astype(jnp.float32)
    second = buffer[step, 1].astype(jnp.float32)
    even = (first + second).reshape(channels * segs, width).astype(jnp.bfloat16)
    odd = (first - second).reshape(channels * segs, width).astype(jnp.bfloat16)
    even_part = jnp.dot(even, table_ref[:, :bins], preferred_element_type=jnp.float32)
    odd_part = jnp.dot(odd, table_ref[:, bins:], preferred_element_type=jnp.float32)
    half_tiles = lane_tiles // 2

    def part_of(tile):
        part = even_part if tile < half_tiles else odd_part
        at = tile % half_tiles * 128
        return part[:, at : at + 128]

    @pl.when(step == 0)
    def _():
        for tile in range(lane_tiles):
            acc[tile] = part_of(tile)

    @pl.when(step > 0)
    def _():
        for tile in range(lane_tiles):
            acc[tile] += part_of(tile)

    @pl.when(step == pl.num_programs(0) - 1)
    def _():
        quarter = lane_tiles // 4
        reals = [*range(quarter), *range(2 * quarter, 3 * quarter)]
        for seg in range(segs):
            rows = pl.ds(seg, channels, stride=segs)
            power_sum = None
            for tile in reals:
                real, imag = acc[tile, rows, :], acc[tile + quarter, rows, :]
                power = real * real + imag * imag
                power_sum = power if power_sum is None else power_sum + power
            water = jnp.sum(power_sum, axis=1, keepdims=True) * (1.0 / bins)
            usable = valid_ref[0, first_seg + seg].astype(jnp.float32)
            for place, tile in enumerate(reals):
                real, imag = acc[tile, rows, :], acc[tile + quarter, rows, :]
                power = real * real + imag * imag
                scale = lax.rsqrt(power + 0.1 * water + 1e-06) * usable
                at = place * 128
                group = segs // len(white_refs)
                white_ref = white_refs[seg // group].at[seg % group]
                white_ref[:, at : at + 128] = (real * scale).astype(jnp.bfloat16)
                white_ref[:, bins + at : bins + at + 128] = (imag * scale).astype(jnp.bfloat16)


def whitened(records, valid_mask, table, first_seg, groups, group):
    channels, segs, samples = records.shape
    width = samples // 2 // STEPS
    rows = groups * group * channels
    return pl.pallas_call(
        functools.partial(spectra_kernel, first_seg=first_seg),
        name="spectra",
        grid_spec=pltpu.PrefetchScalarGridSpec(
            num_scalar_prefetch=1,
            grid=(STEPS,),
            in_specs=[
                pl.BlockSpec(memory_space=pltpu.HBM),
                pl.BlockSpec((width, 2 * BINS), lambda k, valid: (k, 0)),
            ],
            out_specs=[pl.BlockSpec((group, channels, 2 * BINS), lambda k, valid: (0, 0, 0))]
            * groups,
            scratch_shapes=[
                pltpu.VMEM((2 * BINS // 128, rows, 128), jnp.float32),
                pltpu.VMEM((STEPS, 2, channels, groups * group, width), jnp.bfloat16),
                pltpu.SemaphoreType.DMA((STEPS, 2)),
            ],
        ),
        out_shape=[jax.ShapeDtypeStruct((group, channels, 2 * BINS), jnp.bfloat16)] * groups,
        compiler_params=pltpu.CompilerParams(vmem_limit_bytes=56 << 20),
        cost_estimate=pl.CostEstimate(
            flops=4 * rows * samples * BINS,
            bytes_accessed=2 * channels * segs * samples + 2 * samples * BINS,
            transcendentals=rows * BINS,
        ),
    )(valid_mask, records, table)


CH_TILE = 16
TILES = 2
WINDOW = 13


def cross_kernel(band_ref, rank_ref, *rest, groups, specs, quarters, first, last):
    if last:
        scale_ref, *rest = rest
    parts, segs = len(groups), sum(groups)
    sources, rest = rest[: 3 * parts], rest[3 * parts :]
    lag_hbm, *rest = rest
    if not first:
        before_hbm, *rest = rest
    count = len(quarters) if last else 1
    outs, rest = rest[:count], rest[count:]
    extended, lag_ref, wide, before, in_sems, out_sems, *results = rest
    if last:
        turned, *results = results
    columns = extended.shape[2]
    channels = extended.shape[1] // (REACH + 1)
    lane_tiles = columns // 256
    steps = channels // (TILES * CH_TILE)
    lowest, highest, rank = band_ref[0, 0], band_ref[0, 1], rank_ref[0]
    starts = [8 * (rank ^ flip) for flip in (0, 2, 1, 3)]
    origin = lowest // CH_TILE * CH_TILE

    loads = []
    for number, source in enumerate(sources):
        hop, part = divmod(number, parts)
        into = pl.ds(sum(groups[:part]), groups[part])
        into = extended.at[into, pl.ds(hop * channels, channels), :]
        loads.append(pltpu.make_async_copy(source, into, in_sems.at[number]))
    loads.append(pltpu.make_async_copy(lag_hbm, lag_ref, in_sems.at[3 * parts]))
    if not first:
        earlier = pltpu.make_async_copy(before_hbm, before, in_sems.at[3 * parts + 1])
    for load in loads:
        load.start()
    if not first:
        earlier.start()
    for load in loads:
        load.wait()

    def one_window(index, carry):
        row = jnp.minimum(origin + index * CH_TILE, (REACH + 1) * channels - CH_TILE)
        rows = pl.ds(pl.multiple_of(row, CH_TILE), CH_TILE)
        into = pl.ds(pl.multiple_of(index * CH_TILE, CH_TILE), CH_TILE)
        for seg in range(segs):
            for lane in range(2 * lane_tiles):
                block = extended[seg, rows, lane * 128 : lane * 128 + 128]
                wide[seg * 2 * lane_tiles + lane, into, :] = block.astype(jnp.float32)
        return carry

    lax.fori_loop(0, WINDOW, one_window, 0)
    if not first:
        earlier.wait()

    def stores(step):
        rows = pl.ds(pl.multiple_of(step * TILES * CH_TILE, TILES * CH_TILE), TILES * CH_TILE)
        if last:
            picks = [(rows,)] * len(results)
        else:
            picks = [(pl.ds(step * TILES, TILES),)]
        return [
            pltpu.make_async_copy(result.at[pick], out.at[pick], out_sems.at[step, number])
            for number, (result, out, pick) in enumerate(zip(results, outs, picks))
        ]

    def one_step(step, sums):
        bases = [
            pl.multiple_of((step * TILES + tile) * CH_TILE, CH_TILE) for tile in range(TILES)
        ]
        for lane in range(lane_tiles):
            for unit in range(2):
                pltpu.matmul_push_rhs(lag_ref[lane], 0, unit)
            mine = {}
            for tile in range(TILES):
                for seg in range(segs):
                    for part in range(2):
                        at = (part * lane_tiles + lane) * 128
                        rows = pl.ds(bases[tile], CH_TILE)
                        block = extended[seg, rows, at : at + 128].astype(jnp.float32)
                        mine[tile, 0, seg, part] = block[:8]
                        mine[tile, 1, seg, part] = block[8:]
            for pair in range(8 * len(quarters)):
                quarter = quarters[pair // 8]
                offset = (lowest - origin) + starts[quarter] + pair % 8
                for tile in range(TILES):
                    reals, imags = [], []
                    for half in range(2):
                        real = imag = None
                        for seg in range(segs):
                            slab = seg * 2 * lane_tiles + lane
                            rows = pl.ds(bases[tile] + offset + 8 * half, 8)
                            their_real = wide[slab, rows, :]
                            their_imag = wide[slab + lane_tiles, rows, :]
                            my_real = mine[tile, half, seg, 0]
                            my_imag = mine[tile, half, seg, 1]
                            re = my_real * their_real + my_imag * their_imag
                            im = my_imag * their_real - my_real * their_imag
                            real = re if real is None else real + re
                            imag = im if imag is None else imag + im
                        reals.append(real)
                        imags.append(imag)
                    mixed = [
                        jnp.concatenate(part, axis=0).astype(jnp.bfloat16)
                        for part in (reals, imags)
                    ]
                    pltpu.matmul_acc_lhs(
                        sums[TILES * pair + tile],
                        jnp.concatenate(mixed, axis=1),
                        load_staged_rhs=0 if pair == 0 else None,
                    )
        for tile in range(TILES):
            finish(step * TILES + tile, bases[tile], sums[tile::TILES])
        for store in stores(step):
            store.start()

    def finish(tile, base, sums):
        near = lax.broadcasted_iota(jnp.int32, (CH_TILE, LAGS), 0)
        for pair in range(8 * len(quarters)):
            quarter = quarters[pair // 8]
            at = pair * CH_TILE
            rows = slice(at, at + CH_TILE)
            lagged = pltpu.matmul_pop(sums[pair])[:, :LAGS]
            if not first:
                lagged += before[tile, rows].astype(jnp.float32)
            if not last:
                results[0][tile, rows] = lagged.astype(jnp.bfloat16)
                continue
            offset = lowest + starts[quarter] + pair % 8
            partner = near + (base + offset)
            scale = jnp.where(
                partner < channels,
                scale_ref[0],
                jnp.where(partner < 2 * channels, scale_ref[1], scale_ref[2]),
            )
            inside = jnp.where(offset < highest, 1.0, 0.0)
            turned[pair // 8, pl.ds(pair % 8, CH_TILE, stride=8), :] = lagged * (scale * inside)
        if last:
            shape = (CH_TILE, 8, LAGS)
            rows = pl.ds(base, CH_TILE)
            for number, result in enumerate(results):
                result[rows] = turned[number].reshape(shape).astype(result.dtype)

    def all_steps(*sums):
        def body(step, carry):
            one_step(step, sums)
            return carry

        lax.fori_loop(0, steps, body, 0)

    pl.run_scoped(all_steps, *specs)

    def drain(step, carry):
        for store in stores(step):
            store.wait()
        return carry

    lax.fori_loop(0, steps, drain, 0)


def correlated(
    mesh, places, scales, owns, nexts, fars, lag_table, before, quarters, last
):
    groups = [own.shape[0] for own in owns]
    segs = sum(groups)
    _, channels, columns = owns[0].shape
    steps = channels // (TILES * CH_TILE)
    raw_shape = (channels // CH_TILE, 8 * 3 * CH_TILE, LAGS)
    if last:
        out_shape = [
            jax.ShapeDtypeStruct((channels, 8, LAGS), jnp.float32 if q < 2 else jnp.bfloat16)
            for q in quarters
        ]
    else:
        out_shape = [jax.ShapeDtypeStruct(raw_shape, jnp.bfloat16)]
    scratch = [
        pltpu.VMEM((segs, (REACH + 1) * channels, columns), jnp.bfloat16),
        pltpu.VMEM(lag_table.shape, lag_table.dtype),
        pltpu.VMEM((segs * columns // 128, WINDOW * CH_TILE, 128), jnp.float32),
        pltpu.VMEM((8, 128) if before is None else raw_shape, jnp.bfloat16),
        pltpu.SemaphoreType.DMA((3 * len(owns) + 2,)),
        pltpu.SemaphoreType.DMA((steps, 3)),
        *([pltpu.VMEM((len(quarters), CH_TILE * 8, LAGS), jnp.float32)] if last else []),
        *[pltpu.VMEM(shape.shape, shape.dtype) for shape in out_shape],
    ]
    with jax.sharding.use_abstract_mesh(mesh.abstract_mesh):
        specs = [
            pltpu.ACC(tile)((CH_TILE, 256), jnp.float32)
            for _ in range(8 * len(quarters))
            for tile in range(TILES)
        ]
    smem = pl.BlockSpec(memory_space=pltpu.SMEM)
    anywhere = pl.BlockSpec(memory_space=pltpu.HBM)
    small = [*places, scales] if last else places
    large = [*owns, *nexts, *fars, lag_table, *([] if before is None else [before])]
    return pl.pallas_call(
        functools.partial(
            cross_kernel,
            groups=groups,
            specs=specs,
            quarters=quarters,
            first=before is None,
            last=last,
        ),
        name="cross",
        in_specs=[smem] * len(small) + [anywhere] * len(large),
        out_specs=[anywhere] * len(out_shape),
        out_shape=out_shape,
        scratch_shapes=scratch,
        compiler_params=pltpu.CompilerParams(vmem_limit_bytes=60 << 20),
        cost_estimate=pl.CostEstimate(
            flops=20 * channels * 8 * len(quarters) * columns * LAGS,
            bytes_accessed=6 * segs * channels * columns,
            transcendentals=0,
        ),
    )(*small, *large)


def shards(mesh, records, valid_mask, band_limits):
    channels, segs, samples = records.shape
    blocks = lax.axis_size("chan")
    block = lax.axis_index("chan")
    rank = lax.axis_index("tm")[None]

    hop_far = [(i + 2, i) for i in range(blocks - 2)]
    hop_near = [(i + 1, i) for i in range(blocks - 1)]
    pair_swap = [(i ^ 1, i) for i in range(blocks)]
    core_swap = [(i, i ^ 1) for i in range(4)]
    side_swap = [(i, i ^ 2) for i in range(4)]

    lag_table = jnp.asarray(lag_table_of(samples, BINS, LAGS))
    table = jnp.asarray(dft_table_of(samples, BINS))
    half = segs // 2
    whites = [
        *whitened(records, valid_mask, table, 0, 1, half),
        *whitened(records, valid_mask, table, half, half, 1),
    ]
    fars = [lax.ppermute(white, "chan", hop_far) for white in whites]
    valid_mask, _ = lax.optimization_barrier((valid_mask, whites[1]))
    marks = [valid_mask] + [lax.ppermute(valid_mask, "chan", hop) for hop in (hop_near, hop_far)]
    counts = None
    nexts = []
    for white, far in zip(whites, fars):
        if nexts:
            far, _ = lax.optimization_barrier((far, (passed, counts)))
        passed = jnp.where(block % 2 == 0, far, white)
        if not nexts:
            marks, _ = lax.optimization_barrier((marks, passed))
            counts = jnp.sum(jnp.stack(marks) * marks[0][None], axis=(1, 2))
            counts += lax.ppermute(counts, "tm", core_swap)
            counts += lax.ppermute(counts, "tm", side_swap)
        nexts.append(lax.ppermute(passed, "chan", pair_swap))
    scales = 1.0 / jnp.maximum(counts, 1).astype(jnp.float32)

    def stacked(part, quarters, before=None, last=True):
        chosen = (whites[part], nexts[part], fars[part])
        return correlated(mesh, [band_limits, rank], scales, *chosen, lag_table, before, quarters, last)

    (before,) = stacked(slice(0, 1), (1, 3, 2), last=False)
    other, send_far, send = stacked(slice(1, None), (1, 3, 2), before)
    got_far = lax.ppermute(send_far, "tm", core_swap)
    got = lax.ppermute(send, "tm", core_swap)
    passing = (other + got_far.astype(jnp.float32)).astype(jnp.bfloat16)
    crossed = lax.ppermute(passing, "tm", side_swap)
    scales, _ = lax.optimization_barrier((scales, passing))
    (keep,) = stacked(slice(None), (0,))
    return keep + got.astype(jnp.float32) + crossed.astype(jnp.float32)


def solution(mesh):
    placed = (P("chan", "tm", None), P("chan", "tm"), P("chan", None))
    return jax.shard_map(
        functools.partial(shards, mesh),
        mesh=mesh,
        in_specs=placed,
        out_specs=P("chan", "tm", None),
        check_vma=False,
    )
```

```python
import functools
import math

import jax
import jax.numpy as jnp
import numpy as np
from jax import lax
from jax.experimental import pallas as pl
from jax.experimental.pallas import tpu as pltpu
from jax.sharding import PartitionSpec as P

BINS = 512
LAGS = 128
PAIRS = 32
REACH = 2
STEPS = 3


def bin_order(bins):
    return np.concatenate([np.arange(0, bins, 2), np.arange(1, bins, 2)])


def dft_table_of(samples, bins):
    times = np.arange(samples // 2, dtype=np.int64)[:, None]
    freqs = 32 + bin_order(bins)[None, :]
    phase = (times * freqs % samples) * (2.0 * math.pi / samples)
    half = bins // 2
    real, imag = np.cos(phase), -np.sin(phase)
    parts = [real[:, :half], imag[:, :half], real[:, half:], imag[:, half:]]
    return np.concatenate(parts, axis=1).astype(jnp.bfloat16)


def lag_table_of(samples, bins, lags):
    freqs = 32 + bin_order(bins)[:, None]
    shifts = (np.arange(lags) - lags // 2 + samples) % samples
    phase = (freqs * shifts[None, :] % samples) * (2.0 * math.pi / samples)
    factor = 1.0 / math.sqrt(bins)
    parts = np.stack([np.cos(phase), -np.sin(phase)]) * factor
    tiles = parts.reshape(2, bins // 128, 128, lags).transpose(1, 0, 2, 3)
    tiles = tiles.reshape(bins // 128, 256, lags)
    return np.pad(tiles, ((0, 0), (0, 0), (0, 256 - lags))).astype(jnp.bfloat16)


def spectra_kernel(valid_ref, records_hbm, table_ref, *rest, first_seg):
    *white_refs, acc, buffer, sems = rest
    step = pl.program_id(0)
    steps, _, channels, _, width = buffer.shape
    lane_tiles = acc.shape[0]
    bins = table_ref.shape[1] // 2
    segs = acc.shape[1] // channels

    def loads(at):
        copies = []
        for side in range(2):
            columns = pl.ds(pl.multiple_of((at + side * steps) * width, 128), width)
            source = records_hbm.at[:, first_seg : first_seg + segs, columns]
            copies.append(
                pltpu.make_async_copy(source, buffer.at[at, side], sems.at[at, side])
            )
        return copies

    @pl.when(step == 0)
    def _():
        for load in loads(0) + loads(1):
            load.start()

    @pl.when(step + 2 < steps)
    def _():
        for load in loads(step + 2):
            load.start()

    for load in loads(step):
        load.wait()
    first = buffer[step, 0].astype(jnp.float32)
    second = buffer[step, 1].astype(jnp.float32)
    even = (first + second).reshape(channels * segs, width).astype(jnp.bfloat16)
    odd = (first - second).reshape(channels * segs, width).astype(jnp.bfloat16)
    even_part = jnp.dot(even, table_ref[:, :bins], preferred_element_type=jnp.float32)
    odd_part = jnp.dot(odd, table_ref[:, bins:], preferred_element_type=jnp.float32)
    half_tiles = lane_tiles // 2

    def part_of(tile):
        part = even_part if tile < half_tiles else odd_part
        at = tile % half_tiles * 128
        return part[:, at : at + 128]

    @pl.when(step == 0)
    def _():
        for tile in range(lane_tiles):
            acc[tile] = part_of(tile)

    @pl.when(step > 0)
    def _():
        for tile in range(lane_tiles):
            acc[tile] += part_of(tile)

    @pl.when(step == pl.num_programs(0) - 1)
    def _():
        quarter = lane_tiles // 4
        reals = [*range(quarter), *range(2 * quarter, 3 * quarter)]
        for seg in range(segs):
            rows = pl.ds(seg, channels, stride=segs)
            power_sum = None
            for tile in reals:
                real, imag = acc[tile, rows, :], acc[tile + quarter, rows, :]
                power = real * real + imag * imag
                power_sum = power if power_sum is None else power_sum + power
            water = jnp.sum(power_sum, axis=1, keepdims=True) * (1.0 / bins)
            usable = valid_ref[0, first_seg + seg].astype(jnp.float32)
            for place, tile in enumerate(reals):
                real, imag = acc[tile, rows, :], acc[tile + quarter, rows, :]
                power = real * real + imag * imag
                scale = lax.rsqrt(power + 0.1 * water + 1e-06) * usable
                at = place * 128
                group = segs // len(white_refs)
                white_ref = white_refs[seg // group].at[seg % group]
                white_ref[:, at : at + 128] = (real * scale).astype(jnp.bfloat16)
                white_ref[:, bins + at : bins + at + 128] = (imag * scale).astype(jnp.bfloat16)


def whitened(records, valid_mask, table, first_seg, groups, group):
    channels, segs, samples = records.shape
    width = samples // 2 // STEPS
    rows = groups * group * channels
    return pl.pallas_call(
        functools.partial(spectra_kernel, first_seg=first_seg),
        name="spectra",
        grid_spec=pltpu.PrefetchScalarGridSpec(
            num_scalar_prefetch=1,
            grid=(STEPS,),
            in_specs=[
                pl.BlockSpec(memory_space=pltpu.HBM),
                pl.BlockSpec((width, 2 * BINS), lambda k, valid: (k, 0)),
            ],
            out_specs=[pl.BlockSpec((group, channels, 2 * BINS), lambda k, valid: (0, 0, 0))]
            * groups,
            scratch_shapes=[
                pltpu.VMEM((2 * BINS // 128, rows, 128), jnp.float32),
                pltpu.VMEM((STEPS, 2, channels, groups * group, width), jnp.bfloat16),
                pltpu.SemaphoreType.DMA((STEPS, 2)),
            ],
        ),
        out_shape=[jax.ShapeDtypeStruct((group, channels, 2 * BINS), jnp.bfloat16)] * groups,
        compiler_params=pltpu.CompilerParams(vmem_limit_bytes=56 << 20),
        cost_estimate=pl.CostEstimate(
            flops=4 * rows * samples * BINS,
            bytes_accessed=2 * channels * segs * samples + 2 * samples * BINS,
            transcendentals=rows * BINS,
        ),
    )(valid_mask, records, table)


CH_TILE = 16
TILES = 2
WINDOW = 13


def cross_kernel(band_ref, rank_ref, *rest, groups, specs, quarters, first, last):
    if last:
        scale_ref, *rest = rest
    parts, segs = len(groups), sum(groups)
    sources, rest = rest[: 3 * parts], rest[3 * parts :]
    lag_hbm, *rest = rest
    if not first:
        before_hbm, *rest = rest
    count = len(quarters) if last else 1
    outs, rest = rest[:count], rest[count:]
    extended, lag_ref, wide, before, in_sems, out_sems, *results = rest
    if last:
        turned, *results = results
    columns = extended.shape[2]
    channels = extended.shape[1] // (REACH + 1)
    lane_tiles = columns // 256
    steps = channels // (TILES * CH_TILE)
    lowest, highest, rank = band_ref[0, 0], band_ref[0, 1], rank_ref[0]
    starts = [8 * (rank ^ flip) for flip in (0, 2, 1, 3)]
    origin = lowest // CH_TILE * CH_TILE

    loads = []
    for number, source in enumerate(sources):
        hop, part = divmod(number, parts)
        into = pl.ds(sum(groups[:part]), groups[part])
        into = extended.at[into, pl.ds(hop * channels, channels), :]
        loads.append(pltpu.make_async_copy(source, into, in_sems.at[number]))
    loads.append(pltpu.make_async_copy(lag_hbm, lag_ref, in_sems.at[3 * parts]))
    if not first:
        earlier = pltpu.make_async_copy(before_hbm, before, in_sems.at[3 * parts + 1])
    for load in loads:
        load.start()
    if not first:
        earlier.start()
    for load in loads:
        load.wait()

    def one_window(index, carry):
        row = jnp.minimum(origin + index * CH_TILE, (REACH + 1) * channels - CH_TILE)
        rows = pl.ds(pl.multiple_of(row, CH_TILE), CH_TILE)
        into = pl.ds(pl.multiple_of(index * CH_TILE, CH_TILE), CH_TILE)
        for seg in range(segs):
            for lane in range(2 * lane_tiles):
                block = extended[seg, rows, lane * 128 : lane * 128 + 128]
                wide[seg * 2 * lane_tiles + lane, into, :] = block.astype(jnp.float32)
        return carry

    lax.fori_loop(0, WINDOW, one_window, 0)
    if not first:
        earlier.wait()

    def stores(step):
        rows = pl.ds(pl.multiple_of(step * TILES * CH_TILE, TILES * CH_TILE), TILES * CH_TILE)
        if last:
            picks = [(rows,)] * len(results)
        else:
            picks = [(pl.ds(step * TILES, TILES),)]
        return [
            pltpu.make_async_copy(result.at[pick], out.at[pick], out_sems.at[step, number])
            for number, (result, out, pick) in enumerate(zip(results, outs, picks))
        ]

    def one_step(step, sums):
        bases = [
            pl.multiple_of((step * TILES + tile) * CH_TILE, CH_TILE) for tile in range(TILES)
        ]
        for lane in range(lane_tiles):
            for unit in range(2):
                pltpu.matmul_push_rhs(lag_ref[lane], 0, unit)
            mine = {}
            for tile in range(TILES):
                for seg in range(segs):
                    for part in range(2):
                        at = (part * lane_tiles + lane) * 128
                        rows = pl.ds(bases[tile], CH_TILE)
                        block = extended[seg, rows, at : at + 128].astype(jnp.float32)
                        mine[tile, 0, seg, part] = block[:8]
                        mine[tile, 1, seg, part] = block[8:]
            for pair in range(8 * len(quarters)):
                quarter = quarters[pair // 8]
                offset = (lowest - origin) + starts[quarter] + pair % 8
                for tile in range(TILES):
                    reals, imags = [], []
                    for half in range(2):
                        real = imag = None
                        for seg in range(segs):
                            slab = seg * 2 * lane_tiles + lane
                            rows = pl.ds(bases[tile] + offset + 8 * half, 8)
                            their_real = wide[slab, rows, :]
                            their_imag = wide[slab + lane_tiles, rows, :]
                            my_real = mine[tile, half, seg, 0]
                            my_imag = mine[tile, half, seg, 1]
                            re = my_real * their_real + my_imag * their_imag
                            im = my_imag * their_real - my_real * their_imag
                            real = re if real is None else real + re
                            imag = im if imag is None else imag + im
                        reals.append(real)
                        imags.append(imag)
                    mixed = [
                        jnp.concatenate(part, axis=0).astype(jnp.bfloat16)
                        for part in (reals, imags)
                    ]
                    pltpu.matmul_acc_lhs(
                        sums[TILES * pair + tile],
                        jnp.concatenate(mixed, axis=1),
                        load_staged_rhs=0 if pair == 0 else None,
                    )
        for tile in range(TILES):
            finish(step * TILES + tile, bases[tile], sums[tile::TILES])
        for store in stores(step):
            store.start()

    def finish(tile, base, sums):
        near = lax.broadcasted_iota(jnp.int32, (CH_TILE, LAGS), 0)
        for pair in range(8 * len(quarters)):
            quarter = quarters[pair // 8]
            at = pair * CH_TILE
            rows = slice(at, at + CH_TILE)
            lagged = pltpu.matmul_pop(sums[pair])[:, :LAGS]
            if not first:
                lagged += before[tile, rows].astype(jnp.float32)
            if not last:
                results[0][tile, rows] = lagged.astype(jnp.bfloat16)
                continue
            offset = lowest + starts[quarter] + pair % 8
            partner = near + (base + offset)
            scale = jnp.where(
                partner < channels,
                scale_ref[0],
                jnp.where(partner < 2 * channels, scale_ref[1], scale_ref[2]),
            )
            inside = jnp.where(offset < highest, 1.0, 0.0)
            turned[pair // 8, pl.ds(pair % 8, CH_TILE, stride=8), :] = lagged * (scale * inside)
        if last:
            shape = (CH_TILE, 8, LAGS)
            rows = pl.ds(base, CH_TILE)
            for number, result in enumerate(results):
                result[rows] = turned[number].reshape(shape).astype(result.dtype)

    def all_steps(*sums):
        def body(step, carry):
            one_step(step, sums)
            return carry

        lax.fori_loop(0, steps, body, 0)

    pl.run_scoped(all_steps, *specs)

    def drain(step, carry):
        for store in stores(step):
            store.wait()
        return carry

    lax.fori_loop(0, steps, drain, 0)


def correlated(
    mesh, places, scales, owns, nexts, fars, lag_table, before, quarters, last
):
    groups = [own.shape[0] for own in owns]
    segs = sum(groups)
    _, channels, columns = owns[0].shape
    steps = channels // (TILES * CH_TILE)
    raw_shape = (channels // CH_TILE, 8 * 3 * CH_TILE, LAGS)
    if last:
        out_shape = [
            jax.ShapeDtypeStruct((channels, 8, LAGS), jnp.float32 if q < 2 else jnp.bfloat16)
            for q in quarters
        ]
    else:
        out_shape = [jax.ShapeDtypeStruct(raw_shape, jnp.bfloat16)]
    scratch = [
        pltpu.VMEM((segs, (REACH + 1) * channels, columns), jnp.bfloat16),
        pltpu.VMEM(lag_table.shape, lag_table.dtype),
        pltpu.VMEM((segs * columns // 128, WINDOW * CH_TILE, 128), jnp.float32),
        pltpu.VMEM((8, 128) if before is None else raw_shape, jnp.bfloat16),
        pltpu.SemaphoreType.DMA((3 * len(owns) + 2,)),
        pltpu.SemaphoreType.DMA((steps, 3)),
        *([pltpu.VMEM((len(quarters), CH_TILE * 8, LAGS), jnp.float32)] if last else []),
        *[pltpu.VMEM(shape.shape, shape.dtype) for shape in out_shape],
    ]
    with jax.sharding.use_abstract_mesh(mesh.abstract_mesh):
        specs = [
            pltpu.ACC(tile)((CH_TILE, 256), jnp.float32)
            for _ in range(8 * len(quarters))
            for tile in range(TILES)
        ]
    smem = pl.BlockSpec(memory_space=pltpu.SMEM)
    anywhere = pl.BlockSpec(memory_space=pl.ANY)
    small = [*places, scales] if last else places
    large = [*owns, *nexts, *fars, lag_table, *([] if before is None else [before])]
    return pl.pallas_call(
        functools.partial(
            cross_kernel,
            groups=groups,
            specs=specs,
            quarters=quarters,
            first=before is None,
            last=last,
        ),
        name="cross",
        in_specs=[smem] * len(small) + [anywhere] * len(large),
        out_specs=[anywhere] * len(out_shape),
        out_shape=out_shape,
        scratch_shapes=scratch,
        compiler_params=pltpu.CompilerParams(vmem_limit_bytes=24 << 20),
        cost_estimate=pl.CostEstimate(
            flops=20 * channels * 8 * len(quarters) * columns * LAGS,
            bytes_accessed=6 * segs * channels * columns,
            transcendentals=0,
        ),
    )(*small, *large)


def shards(mesh, records, valid_mask, band_limits):
    channels, segs, samples = records.shape
    blocks = lax.axis_size("chan")
    block = lax.axis_index("chan")
    rank = lax.axis_index("tm")[None]

    hop_far = [(i + 2, i) for i in range(blocks - 2)]
    hop_near = [(i + 1, i) for i in range(blocks - 1)]
    pair_swap = [(i ^ 1, i) for i in range(blocks)]
    core_swap = [(i, i ^ 1) for i in range(4)]
    side_swap = [(i, i ^ 2) for i in range(4)]

    lag_table = jnp.asarray(lag_table_of(samples, BINS, LAGS))
    table = jnp.asarray(dft_table_of(samples, BINS))
    half = segs // 2
    whites = [
        *whitened(records, valid_mask, table, 0, 1, half),
        *whitened(records, valid_mask, table, half, half, 1),
    ]
    fars = [lax.ppermute(white, "chan", hop_far) for white in whites]
    valid_mask, _ = lax.optimization_barrier((valid_mask, whites[1]))
    marks = [valid_mask] + [lax.ppermute(valid_mask, "chan", hop) for hop in (hop_near, hop_far)]
    counts = None
    nexts = []
    for white, far in zip(whites, fars):
        if nexts:
            far, _ = lax.optimization_barrier((far, (passed, counts)))
        passed = jnp.where(block % 2 == 0, far, white)
        if not nexts:
            marks, _ = lax.optimization_barrier((marks, passed))
            counts = jnp.sum(jnp.stack(marks) * marks[0][None], axis=(1, 2))
            counts += lax.ppermute(counts, "tm", core_swap)
            counts += lax.ppermute(counts, "tm", side_swap)
        nexts.append(lax.ppermute(passed, "chan", pair_swap))
    scales = 1.0 / jnp.maximum(counts, 1).astype(jnp.float32)

    def stacked(part, quarters, before=None, last=True):
        chosen = (whites[part], nexts[part], fars[part])
        return correlated(mesh, [band_limits, rank], scales, *chosen, lag_table, before, quarters, last)

    (before,) = stacked(slice(0, 1), (1, 3, 2), last=False)
    other, send_far, send = stacked(slice(1, None), (1, 3, 2), before)
    got_far = lax.ppermute(send_far, "tm", core_swap)
    got = lax.ppermute(send, "tm", core_swap)
    passing = (other + got_far.astype(jnp.float32)).astype(jnp.bfloat16)
    crossed = lax.ppermute(passing, "tm", side_swap)
    scales, _ = lax.optimization_barrier((scales, passing))
    (keep,) = stacked(slice(None), (0,))
    return keep + got.astype(jnp.float32) + crossed.astype(jnp.float32)


def solution(mesh):
    placed = (P("chan", "tm", None), P("chan", "tm"), P("chan", None))
    return jax.shard_map(
        functools.partial(shards, mesh),
        mesh=mesh,
        in_specs=placed,
        out_specs=P("chan", "tm", None),
        check_vma=False,
    )
```
